512 devices in a mesh: feat: 32 (over x, y, core), rep: 16 (over z).
Axes of the slice: x: 4, y: 4, z: 16, core: 2. Of those that a mesh axis runs over, the one named last changes fastest.
Arguments:
- feats: bfloat16 [16, 8192, 1024], P('rep', None, 'feat'), may hold values from -6 to 6
- w_self: bfloat16 [1024, 256], P('feat'), may hold values from -0.1875 to 0.1875
- w_neigh: bfloat16 [1024, 256], P('feat'), may hold values from -0.1875 to 0.1875
- bias: float32 [256], replicated, may hold values from -3 to 3
- tile_weight: bfloat16 [16, 32, 3, 128, 128], P('rep'), may hold values from -0.375 to 0.375
- tile_src: int32 [16, 32, 3], P('rep'), may hold values from 0 to 63
- tile_count: int32 [16, 32], P('rep'), may hold values from 1 to 3
- owner_order: int32 [16, 32], P('rep'), may hold values from 0 to 31, each once within a row
- cotangent: bfloat16 [16, 4096, 256], P('rep', 'feat'), may hold values from -6 to 6
Outputs:
- hidden: bfloat16 [16, 4096, 256], P('rep', 'feat')
- grad_self: float32 [1024, 256], P('feat')
- grad_neigh: float32 [1024, 256], P('feat')
The draws below stay inside these ranges and needn't reach their ends.
All inputs are finite; a program needn't handle non-finite values.
Results may differ from the reference program's by a relative error of at most 0.0055.
Values may be sent and summed in bfloat16 or wider, within the bound.
A program may use at most 64 MiB of HBM per device.

```python
import jax
import jax.numpy as jnp
from jax import lax

F = 1024
H = 256
BLOCK = 128
KMAX = 3
NDB = 32
NSB = 64
N_REP = 16


def set_ends(entries, own_key, low, largest):
    shape = entries.shape
    index_at = [jax.random.randint(jax.random.fold_in(own_key, axis), (), 0, shape[axis]) for axis in range(len(shape))]
    entries = entries.at[tuple(index_at)].set(low)
    longest = shape.index(max(shape))
    index_at[longest] = (index_at[longest] + 1) % shape[longest]
    return entries.at[tuple(index_at)].set(largest)


def strengthened(values, rng, source, target, shards_of, factor):
    owner, partner = [(jnp.arange(values.shape[dim]) // (values.shape[dim] // shards_of)).reshape([-1 if axis == dim else 1 for axis in range(values.ndim)]) for dim in (source, target)]
    chosen = jax.random.permutation(rng, shards_of)[partner]
    strong = (owner == chosen) | (owner == (partner + shards_of // 2) % shards_of)
    return jnp.where(strong, factor * values, values)


def shard_levels(stream_key, dims, pieces, low, high):
    loudness, own = 1.0, jax.random.fold_in(stream_key, 6)
    for axis_at, blocks in pieces:
        draws = jnp.exp(jax.random.uniform(jax.random.fold_in(own, axis_at), (blocks,), jnp.float32, low / len(pieces), high / len(pieces)))
        loudness = loudness * jnp.repeat(draws, dims[axis_at] // blocks).reshape([-1 if axis == axis_at else 1 for axis in range(len(dims))])
    return loudness


def centred(own_key, dims, scale, bound, cuts=(), held_as=jnp.bfloat16):
    result = scale * jax.random.normal(own_key, dims, jnp.float32)
    if cuts:
        result = result * shard_levels(own_key, dims, cuts, -0.22, 0.18)
    return jnp.clip(result, -bound, bound).astype(held_as)


def noise_with(rng, extent, scale, reach, pieces, heavy, held_as=jnp.bfloat16):
    entries = scale * jax.random.normal(rng, extent, jnp.float32)
    if pieces:
        entries = entries * shard_levels(rng, extent, pieces, -0.22, 0.18)
    return jnp.clip(strengthened(entries, jax.random.fold_in(rng, 3), *heavy), -reach, reach).astype(held_as)


def setup_inputs(seed: int = 0) -> dict:
    seeds = jax.random.split(jax.random.key(seed), 10)
    feats = noise_with(seeds[0], (N_REP, NSB * BLOCK, F), 1.0, 6.0, ((0, 16), (2, 32)), (2, 1, 32, 2.75))
    w_self = centred(seeds[1], (F, H), F ** -0.5, 0.1875, ((0, 32),))
    w_neigh = centred(seeds[2], (F, H), F ** -0.5, 0.1875, ((0, 32),))
    bias = centred(seeds[3], (H,), 0.5, 3.0, (), jnp.float32)
    tile_weight = centred(seeds[4], (N_REP, NDB, KMAX, BLOCK, BLOCK), 0.0625, 0.375, ((0, 16),))
    tile_src = set_ends(jax.random.randint(seeds[5], (N_REP, NDB, KMAX), 0, NSB), jax.random.fold_in(seeds[5], 1), 0, NSB - 1).astype(jnp.int32)
    tile_count = set_ends(jax.random.randint(seeds[6], (N_REP, NDB), 1, KMAX + 1), jax.random.fold_in(seeds[6], 1), 1, KMAX).astype(jnp.int32)
    owner_order = jax.vmap(lambda own: jax.random.permutation(own, NDB))(jax.random.split(seeds[7], N_REP)).reshape((N_REP, NDB)).astype(jnp.int32)
    cotangent = centred(seeds[8], (N_REP, NDB * BLOCK, H), 1.0, 6.0, ((0, 16), (1, 32)))
    return {"feats": feats, "w_self": w_self, "w_neigh": w_neigh, "bias": bias, "tile_weight": tile_weight, "tile_src": tile_src, "tile_count": tile_count, "owner_order": owner_order, "cotangent": cotangent}


def one_batch(inputs):
    feats, tile_weight, tile_src, tile_count, owner_order, cotangent, w_self, w_neigh, bias = inputs
    by_block = feats.reshape(NSB, BLOCK, F)
    in_use = jnp.arange(KMAX)[None, :] < tile_count[:, None]
    masked = jnp.where(in_use[:, :, None, None], tile_weight, jnp.zeros((), jnp.bfloat16))
    sources = by_block[tile_src]
    aggregate = jnp.einsum("bkij,bkjc->bic", masked.astype(jnp.float32), sources.astype(jnp.float32)).astype(jnp.bfloat16)
    target_rows = by_block[owner_order].reshape(-1, F)
    target_mean = aggregate[owner_order].reshape(-1, F)
    preact = jnp.dot(target_rows, w_self, preferred_element_type=jnp.float32)
    preact = preact + jnp.dot(target_mean, w_neigh, preferred_element_type=jnp.float32) + bias
    hidden = jax.nn.silu(preact).astype(jnp.bfloat16)
    squash = jax.nn.sigmoid(preact)
    output_grad = (cotangent.astype(jnp.float32) * squash * (1.0 + preact * (1.0 - squash))).astype(jnp.bfloat16)
    grad_self = jnp.dot(target_rows.T, output_grad, preferred_element_type=jnp.float32)
    grad_neigh = jnp.dot(target_mean.T, output_grad, preferred_element_type=jnp.float32)
    return hidden, grad_self, grad_neigh


def reference(feats, w_self, w_neigh, bias, tile_weight, tile_src, tile_count, owner_order, cotangent):
    def wrapped(inputs):
        return one_batch(inputs + (w_self, w_neigh, bias))

    hidden, grad_self, grad_neigh = lax.map(wrapped, (feats, tile_weight, tile_src, tile_count, owner_order, cotangent))
    return hidden, jnp.sum(grad_self, axis=0), jnp.sum(grad_neigh, axis=0)
```

```python
import functools

import jax
import jax.numpy as jnp
from jax import lax
from jax.experimental import pallas as pl
from jax.experimental.pallas import tpu as pltpu
from jax.sharding import PartitionSpec as P

MESH = pl.DeviceIdType.MESH
SIDE = 4
PLANE = 2 * SIDE * SIDE
F32 = jnp.float32
BF16 = jnp.bfloat16


def remote(src, dst, send_sem, recv_sem, axis, index):
    return pltpu.make_async_remote_copy(
        src_ref=src,
        dst_ref=dst,
        send_sem=send_sem,
        recv_sem=recv_sem,
        device_id={axis: index},
        device_id_type=MESH,
    )


def exchange_kernel(
    reps,
    slots,
    src_ref,
    count_ref,
    order_ref,
    feats_hbm,
    tiles_hbm,
    w_self_hbm,
    w_neigh_hbm,
    bias_ref,
    cot_ref,
    hidden_ref,
    total_ref,
    feats,
    tiles,
    mine,
    rows,
    weights,
    grads,
    part,
    parts,
    load_sems,
    a2a_send,
    a2a_recv,
    w_send,
    w_recv,
    g_send,
    g_recv,
    z_send,
    z_recv,
    t_send,
    t_recv,
):
    me = lax.axis_index("feat")
    z = lax.axis_index("rep")
    x, y, c = me // (2 * SIDE), (me // 2) % SIDE, me % 2

    loads = [
        pltpu.make_async_copy(w_self_hbm, weights.at[0, pl.ds(0, 32)], load_sems.at[0]),
        pltpu.make_async_copy(w_neigh_hbm, weights.at[0, pl.ds(32, 32)], load_sems.at[1]),
        pltpu.make_async_copy(tiles_hbm, tiles, load_sems.at[2]),
    ]
    for load in loads:
        load.start()

    def load_block(s, carry):
        lanes = pl.ds(pl.multiple_of(s * 128, 128), 128)
        pltpu.make_async_copy(feats_hbm.at[:, lanes], feats.at[s], load_sems.at[3]).start()
        return carry

    lax.fori_loop(0, feats.shape[0], load_block, 0)

    barrier = pltpu.get_barrier_semaphore()

    def greet_plane(d, carry):
        pl.semaphore_signal(
            barrier, inc=1, device_id={"feat": lax.rem(me + d, PLANE)}, device_id_type=MESH
        )
        return carry

    def greet_rep(d, carry):
        pl.semaphore_signal(
            barrier, inc=1, device_id={"rep": lax.rem(z + d, reps)}, device_id_type=MESH
        )
        return carry

    lax.fori_loop(1, reps, greet_rep, 0)
    lax.fori_loop(1, PLANE, greet_plane, 0)

    for load in loads:
        load.wait()
    pltpu.make_async_copy(feats, feats, load_sems.at[3]).wait()

    def combine(p, carry):
        block = order_ref[0, p]
        used = count_ref[0, block]
        total = jnp.zeros((32, 128), F32)
        for k in range(slots):
            product = lax.dot_general(
                feats[src_ref[k, block]],
                tiles[block, k],
                (((1,), (1,)), ((), ())),
                preferred_element_type=F32,
            )
            total = total + product * (k < used).astype(F32)
        mine[p, 0:32, :] = feats[block]
        mine[p, 32:64, :] = total.astype(BF16)
        return carry

    lax.fori_loop(0, PLANE, combine, 0)
    pl.semaphore_wait(barrier, PLANE + reps - 2)

    def at(dx, dy, dc):
        return (
            lax.rem(x + dx, SIDE) * (2 * SIDE) + lax.rem(y + dy, SIDE) * 2 + lax.rem(c + dc, 2)
        )

    first = lambda k: (k * (1 - c) * SIDE + k * c) * 2
    second = lambda k: (k * c * SIDE + k * (1 - c)) * 2
    first_at = lambda k: at(k * (1 - c), k * c, 0)
    second_at = lambda k: at(k * c, k * (1 - c), 0)
    partner = at(0, 0, 1)

    class Gather:
        def __init__(self, buffer, send, recv):
            self.buffer, self.send, self.recv = buffer, send, recv
            self.sent = []

        def go(self, source, target, index):
            copy = remote(
                self.buffer.at[source],
                self.buffer.at[target],
                self.send.at[len(self.sent)],
                self.recv.at[target],
                "feat",
                index,
            )
            copy.start()
            self.sent.append(copy)

        def got(self, slot):
            remote(
                self.buffer.at[slot],
                self.buffer.at[slot],
                self.send.at[0],
                self.recv.at[slot],
                "feat",
                partner,
            ).wait_recv()

        def stage_one(self):
            for k in (1, 3, 2):
                self.go(0, first(k), first_at(k))
                self.go(0, second(k), second_at(k))
            self.go(0, 1, partner)

        def stage_two(self):
            for k in (1, 3, 2):
                self.got(first(k))
                for j in (1, 3, 2):
                    self.go(first(k), first(k) + second(j), second_at(j))
                self.go(first(k), first(k) + 1, partner)
            for k in (1, 3, 2):
                self.got(second(k))
                self.go(second(k), second(k) + 1, partner)

        def stage_three(self):
            for k in (1, 3, 2):
                for j in (1, 3, 2):
                    self.got(first(k) + second(j))
                    self.go(first(k) + second(j), first(k) + second(j) + 1, partner)

        def finish(self):
            for s in range(SIDE * SIDE):
                self.got(2 * s + 1)

        def drain(self):
            for copy in self.sent:
                copy.wait_send()

    w_gather = Gather(weights, w_send, w_recv)
    w_gather.stage_one()

    rows[0] = mine[me]

    def send_rows(d, carry):
        dx, dy, dc = d // (2 * SIDE), (d // 2) % SIDE, d % 2
        target = at(dx, dy, dc)
        remote(mine.at[target], rows.at[d], a2a_send, a2a_recv, "feat", target).start()
        return carry

    lax.fori_loop(1, PLANE, send_rows, 0)
    w_gather.stage_two()
    w_gather.stage_three()
    w_gather.finish()
    every = pl.ds(1, PLANE - 1)
    all_rows = remote(rows.at[every], rows.at[every], a2a_send, a2a_recv, "feat", partner)
    all_rows.wait_recv()

    def forward(g, acc):
        left = rows[pl.ds(4 * g, 4)].reshape(256, 128)
        right = weights[pl.ds(4 * g, 4)].reshape(256, 256)
        return acc + lax.dot_general(
            left, right, (((0,), (0,)), ((), ())), preferred_element_type=F32
        )

    preact = lax.fori_loop(0, PLANE // 4, forward, jnp.zeros((128, 256), F32)) + bias_ref[...]
    squash = jax.nn.sigmoid(preact)
    hidden_ref[...] = (preact * squash).astype(BF16)
    grads[0] = (cot_ref[...].astype(F32) * squash * (1.0 + preact * (1.0 - squash))).astype(BF16)

    g_gather = Gather(grads, g_send, g_recv)
    g_gather.stage_one()
    g_gather.stage_two()
    g_gather.stage_three()
    g_gather.finish()

    def backward(s, acc):
        px = lax.rem(x + SIDE - s // SIDE, SIDE)
        py = lax.rem(y + SIDE - s % SIDE, SIDE)
        base = px * (2 * SIDE) + py * 2
        left = jnp.concatenate([mine[base + c], mine[base + 1 - c]], axis=1)
        right = grads[pl.ds(2 * s, 2)].reshape(256, 256)
        return acc + jnp.dot(left, right, preferred_element_type=F32)

    grad = lax.fori_loop(0, SIDE * SIDE, backward, jnp.zeros((64, 256), F32))
    for row in range(8):
        for col in range(2):
            part[row * 2 + col] = grad[row * 8 : row * 8 + 8, col * 128 : col * 128 + 128]

    def scatter(d, carry):
        target = lax.rem(z + d, reps)
        remote(part.at[target], parts.at[d], z_send, z_recv, "rep", target).start()
        return carry

    lax.fori_loop(1, reps, scatter, 0)
    parts[0] = part[z]
    others = pl.ds(1, reps - 1)
    all_parts = remote(parts.at[others], parts.at[others], z_send, z_recv, "rep", 0)
    all_parts.wait_recv()

    acc = parts[0]
    for d in range(1, reps):
        acc = acc + parts[d]
    total_ref[0] = acc

    def spread(d, carry):
        target = lax.rem(z + d, reps)
        remote(total_ref.at[0], total_ref.at[d], t_send, t_recv, "rep", target).start()
        return carry

    lax.fori_loop(1, reps, spread, 0)
    all_total = remote(total_ref.at[others], total_ref.at[others], t_send, t_recv, "rep", 0)
    all_total.wait_recv()
    all_total.wait_send()
    all_parts.wait_send()
    all_rows.wait_send()
    w_gather.drain()
    g_gather.drain()


def finish_kernel(reps, hidden_in, total_in, hidden_ref, grad_self_ref, grad_neigh_ref):
    z = lax.axis_index("rep")
    hidden_ref[0] = hidden_in[...]
    for piece in range(16):
        row, col = piece // 2, piece % 2
        value = total_in[lax.rem(z + reps - piece, reps)]
        target = grad_self_ref if row < 4 else grad_neigh_ref
        target[row % 4 * 8 : row % 4 * 8 + 8, col * 128 : col * 128 + 128] = value


def solution(mesh):
    reps = mesh.shape["rep"]

    def body(feats, w_self, w_neigh, bias, tile_weight, tile_src, tile_count, owner_order, cotangent):
        slots = tile_weight.shape[2]
        smem = pl.BlockSpec(memory_space=pltpu.SMEM)
        vmem = pl.BlockSpec(memory_space=pltpu.VMEM)
        anywhere = pl.BlockSpec(memory_space=pl.ANY)
        dma = pltpu.SemaphoreType.DMA
        hidden, total = pl.pallas_call(
            functools.partial(exchange_kernel, reps, slots),
            out_shape=(
                jax.ShapeDtypeStruct((128, 256), BF16),
                jax.ShapeDtypeStruct((reps, 8, 128), F32),
            ),
            in_specs=[smem] * 3 + [anywhere] * 4 + [vmem] * 2,
            out_specs=(vmem, vmem),
            scratch_shapes=[
                pltpu.VMEM((64, 32, 128), BF16),
                pltpu.VMEM((32, slots, 128, 128), BF16),
                pltpu.VMEM((PLANE, 64, 128), BF16),
                pltpu.VMEM((PLANE, 64, 128), BF16),
                pltpu.VMEM((PLANE, 64, 256), BF16),
                pltpu.VMEM((PLANE, 128, 256), BF16),
                pltpu.VMEM((reps, 8, 128), F32),
                pltpu.VMEM((reps, 8, 128), F32),
                dma((4,)),
                dma,
                dma,
                dma((PLANE,)),
                dma((PLANE,)),
                dma((PLANE,)),
                dma((PLANE,)),
                dma,
                dma,
                dma,
                dma,
            ],
            compiler_params=pltpu.CompilerParams(collective_id=0, has_side_effects=True),
            name="exchange",
        )(
            tile_src[0].T,
            tile_count,
            owner_order,
            feats[0].T,
            tile_weight[0],
            w_self,
            w_neigh,
            bias.reshape(1, -1),
            cotangent[0],
        )
        return pl.pallas_call(
            functools.partial(finish_kernel, reps),
            out_shape=(
                jax.ShapeDtypeStruct((1, 128, 256), BF16),
                jax.ShapeDtypeStruct((32, 256), F32),
                jax.ShapeDtypeStruct((32, 256), F32),
            ),
            in_specs=[vmem] * 2,
            out_specs=(vmem,) * 3,
            name="finish",
        )(hidden, total)

    in_specs = (
        P("rep", None, "feat"),
        P("feat", None),
        P("feat", None),
        P(),
        P("rep", None, None, None, None),
        P("rep", None, None),
        P("rep", None),
        P("rep", None),
        P("rep", "feat", None),
    )
    out_specs = (P("rep", "feat", None), P("feat", None), P("feat", None))
    return jax.shard_map(body, mesh=mesh, in_specs=in_specs, out_specs=out_specs, check_vma=False)
```

```python
import functools

import jax
import jax.numpy as jnp
from jax import lax
from jax.experimental import pallas as pl
from jax.experimental.pallas import tpu as pltpu
from jax.sharding import PartitionSpec as P

MESH = pl.DeviceIdType.MESH
SIDE = 4
PLANE = 2 * SIDE * SIDE
F32 = jnp.float32
BF16 = jnp.bfloat16


def remote(src, dst, send_sem, recv_sem, axis, index):
    return pltpu.make_async_remote_copy(
        src_ref=src,
        dst_ref=dst,
        send_sem=send_sem,
        recv_sem=recv_sem,
        device_id={axis: index},
        device_id_type=MESH,
    )


def exchange_kernel(
    reps,
    slots,
    src_ref,
    count_ref,
    order_ref,
    feats_hbm,
    tiles_hbm,
    w_self_hbm,
    w_neigh_hbm,
    bias_hbm,
    cot_hbm,
    hidden_out,
    total_out,
    feats,
    tiles,
    means,
    mine,
    rows,
    weights,
    grads,
    cot,
    bias,
    hidden,
    part,
    near,
    far,
    whole,
    load_sems,
    tile_sems,
    out_sems,
    ready_sems,
    a2a_send,
    a2a_recv,
    w_send,
    w_recv,
    g_send,
    g_recv,
    z_send,
    z_recv,
):
    me = lax.axis_index("feat")
    z = lax.axis_index("rep")
    x, y, c = me // (2 * SIDE), (me // 2) % SIDE, me % 2
    blocks = tiles.shape[0]
    chunks = tile_sems.shape[0]
    chunk = blocks // chunks

    barrier = pltpu.get_barrier_semaphore()

    def greet_plane(d, carry):
        pl.semaphore_signal(
            barrier, inc=1, device_id={"feat": lax.rem(me + d, PLANE)}, device_id_type=MESH
        )
        return carry

    lax.fori_loop(1, PLANE, greet_plane, 0)
    for d in range(1, 5):
        for target in (lax.rem(z + d, reps), lax.rem(z + reps - d, reps)):
            pl.semaphore_signal(barrier, inc=1, device_id={"rep": target}, device_id_type=MESH)

    w_loads = [
        pltpu.make_async_copy(w_self_hbm, weights.at[0, pl.ds(0, 32)], load_sems.at[0]),
        pltpu.make_async_copy(w_neigh_hbm, weights.at[0, pl.ds(32, 32)], load_sems.at[1]),
    ]
    for load in w_loads:
        load.start()

    def load_block(s, carry):
        lanes = pl.ds(pl.multiple_of(s * 128, 128), 128)
        pltpu.make_async_copy(feats_hbm.at[:, lanes], feats.at[s], load_sems.at[2]).start()
        return carry

    lax.fori_loop(0, feats.shape[0], load_block, 0)
    tile_loads = []
    for i in range(chunks):
        piece = pl.ds(i * chunk, chunk)
        tile_loads.append(pltpu.make_async_copy(tiles_hbm.at[piece], tiles.at[piece], tile_sems.at[i]))
        tile_loads[-1].start()
    small_loads = [
        pltpu.make_async_copy(bias_hbm, bias, load_sems.at[3]),
        pltpu.make_async_copy(cot_hbm, cot, load_sems.at[4]),
    ]
    for load in small_loads:
        load.start()

    def at(dx, dy, dc):
        return (
            lax.rem(x + dx, SIDE) * (2 * SIDE) + lax.rem(y + dy, SIDE) * 2 + lax.rem(c + dc, 2)
        )

    first = lambda k: (k * (1 - c) * SIDE + k * c) * 2
    second = lambda k: (k * c * SIDE + k * (1 - c)) * 2
    first_at = lambda k: at(k * (1 - c), k * c, 0)
    second_at = lambda k: at(k * c, k * (1 - c), 0)
    partner = at(0, 0, 1)
    near_first = (1, 3, 2)

    class Gather:
        def __init__(self, buffer, send, recv, cuts):
            self.buffer, self.send, self.recv, self.cuts = buffer, send, recv, cuts
            self.height = buffer.shape[1] // cuts
            self.sent = []

        def ref(self, slot, h):
            return self.buffer.at[slot, pl.ds(h * self.height, self.height)]

        def go(self, source, target, h, index):
            copy = remote(
                self.ref(source, h),
                self.ref(target, h),
                self.send.at[len(self.sent)],
                self.recv.at[target * self.cuts + h],
                "feat",
                index,
            )
            copy.start()
            self.sent.append(copy)

        def got(self, slot, h):
            ref = self.ref(slot, h)
            sem = self.recv.at[slot * self.cuts + h]
            remote(ref, ref, self.send.at[0], sem, "feat", partner).wait_recv()

        def stage_one(self):
            for h in range(self.cuts):
                for k in near_first:
                    self.go(0, first(k), h, first_at(k))
            for h in range(self.cuts):
                for k in near_first:
                    self.go(0, second(k), h, second_at(k))
            for h in range(self.cuts):
                self.go(0, 1, h, partner)

        def stage_two(self):
            for h in range(self.cuts):
                for k in near_first:
                    self.got(first(k), h)
                    for j in near_first:
                        self.go(first(k), first(k) + second(j), h, second_at(j))
                    self.go(first(k), first(k) + 1, h, partner)

        def cross(self, slot):
            for h in range(self.cuts):
                self.got(slot, h)
                self.go(slot, slot + 1, h, partner)

        def take(self, slot):
            for h in range(self.cuts):
                self.got(slot, h)

        def drain(self):
            for copy in self.sent:
                copy.wait_send()

    for load in w_loads:
        load.wait()
    pl.semaphore_wait(barrier, PLANE - 1 + 8)
    w_gather = Gather(weights, w_send, w_recv, 1)
    w_gather.stage_one()
    for i, target in enumerate((lax.rem(z + 4, reps), lax.rem(z + reps - 4, reps))):
        pl.semaphore_signal(
            ready_sems.at[i], inc=1, device_id={"rep": target}, device_id_type=MESH
        )

    pltpu.make_async_copy(feats, feats, load_sems.at[2]).wait()
    for b in range(blocks):
        if b % chunk == 0:
            tile_loads[b // chunk].wait()
        used = count_ref[0, b]
        left = jnp.concatenate(
            [feats[src_ref[k, 0, b]] * (k < used).astype(F32).astype(BF16) for k in range(slots)],
            axis=1,
        )
        right = jnp.concatenate([tiles[b, k] for k in range(slots)], axis=1)
        means[b] = lax.dot_general(
            left, right, (((1,), (1,)), ((), ())), preferred_element_type=F32
        ).astype(BF16)

    def arrange(p, carry):
        block = order_ref[0, p]
        mine[p, 0:32, :] = feats[block]
        mine[p, 32:64, :] = means[block]
        return carry

    lax.fori_loop(0, PLANE, arrange, 0, unroll=4)

    w_gather.stage_two()

    def send_rows(d, carry):
        dx, dy, dc = d // (2 * SIDE), (d // 2) % SIDE, d % 2
        target = at(dx, dy, dc)
        remote(
            mine.at[target], rows.at[d], a2a_send, a2a_recv.at[d], "feat", target
        ).start()
        return carry

    lax.fori_loop(1, PLANE, send_rows, 0)
    rows[0] = mine[me]
    for load in small_loads:
        load.wait()

    for k in near_first:
        w_gather.cross(second(k))
    for k in near_first:
        for j in near_first:
            w_gather.cross(first(k) + second(j))
    for s in range(SIDE * SIDE):
        w_gather.take(2 * s + 1)

    preact = jnp.broadcast_to(bias[...], (128, 256))
    for g in (0, 1, 2, 3, 6, 7, 4, 5):
        for d in range(4 * g, 4 * g + 4):
            if d:
                remote(
                    rows.at[d], rows.at[d], a2a_send, a2a_recv.at[d], "feat", partner
                ).wait_recv()
        left = rows[4 * g : 4 * g + 4].reshape(256, 128)
        right = weights[4 * g : 4 * g + 4].reshape(256, 256)
        preact = preact + lax.dot_general(
            left, right, (((0,), (0,)), ((), ())), preferred_element_type=F32
        )
    squash = jax.nn.sigmoid(preact)
    slope = cot[...].astype(F32) * squash * (1.0 + preact * (1.0 - squash))
    grads[0] = slope.astype(BF16)
    g_gather = Gather(grads, g_send, g_recv, 2)
    g_gather.stage_one()
    hidden[...] = (preact * squash).astype(BF16)
    hidden_copy = pltpu.make_async_copy(hidden, hidden_out, out_sems.at[0])
    hidden_copy.start()

    def term(slot):
        dx, dy, dc = slot // (2 * SIDE), (slot // 2) % SIDE, slot % 2
        owner = at(SIDE - dx, SIDE - dy, dc)
        return jnp.dot(mine[owner], grads[slot], preferred_element_type=F32)

    grad = term(0)
    g_gather.stage_two()
    for k in near_first:
        grad = grad + term(first(k))
    for k in near_first:
        g_gather.cross(second(k))
        grad = grad + term(second(k))
    g_gather.take(1)
    grad = grad + term(1)
    for k in near_first:
        for j in near_first:
            g_gather.cross(first(k) + second(j))
            grad = grad + term(first(k) + second(j))
    for k in near_first:
        for side in (second(k), first(k)):
            g_gather.take(side + 1)
            grad = grad + term(side + 1)
    for k in near_first:
        for j in near_first:
            slot = second(k) + first(j) + 1
            g_gather.take(slot)
            grad = grad + term(slot)

    for row in range(8):
        for col in range(2):
            piece = row * 2 + col
            part[piece // 4, piece % 4] = grad[row * 8 : row * 8 + 8, col * 128 : col * 128 + 128]

    sent = []

    def send_rep(source, target, offset):
        copy = remote(
            source,
            target,
            z_send.at[len(sent)],
            z_recv.at[len(sent)],
            "rep",
            lax.rem(z + reps + offset, reps),
        )
        copy.start()
        sent.append(copy)

    for o in (2, 1, -1):
        send_rep(part.at[lax.rem(z + 4 + o, 4)], near.at[o % 4], o)
    for copy in sent[0:3]:
        copy.wait_recv()
    far[z // 4] = (part[lax.rem(z, 4)] + near[2]) + (near[1] + near[3])
    pl.semaphore_wait(ready_sems.at[0], 1)
    pl.semaphore_wait(ready_sems.at[1], 1)
    for o in (8, 4, -4):
        send_rep(far.at[z // 4], far.at[z // 4], o)
    for i, o in enumerate((8, 4, -4)):
        slot = far.at[lax.rem(z + reps - o, reps) // 4]
        remote(slot, slot, z_send.at[3 + i], z_recv.at[3 + i], "rep", z).wait_recv()
    whole[...] = (far[0] + far[1]) + (far[2] + far[3])
    for o in (2, 1, -1):
        send_rep(whole, total_out.at[o % 4], o)
    own = pltpu.make_async_copy(whole, total_out.at[0], out_sems.at[1])
    own.start()

    for copy in sent[0:6]:
        copy.wait_send()
    all_rows = pl.ds(1, PLANE - 1)
    remote(
        mine.at[all_rows], mine.at[all_rows], a2a_send, a2a_recv.at[0], "feat", partner
    ).wait_send()
    w_gather.drain()
    g_gather.drain()
    hidden_copy.wait()
    own.wait()
    for copy in sent[6:9]:
        copy.wait()


def finish_kernel(hidden_in, total_in, hidden_ref, grad_self_ref, grad_neigh_ref):
    z = lax.axis_index("rep")
    hidden_ref[0] = hidden_in[...]
    for piece in range(16):
        row, col = piece // 2, piece % 2
        value = total_in[lax.rem(z + 4 - piece // 4, 4), piece % 4]
        target = grad_self_ref if row < 4 else grad_neigh_ref
        target[row % 4 * 8 : row % 4 * 8 + 8, col * 128 : col * 128 + 128] = value


def solution(mesh):
    reps = mesh.shape["rep"]

    def body(feats, w_self, w_neigh, bias, tile_weight, tile_src, tile_count, owner_order, cotangent):
        slots = tile_weight.shape[2]
        smem = pl.BlockSpec(memory_space=pltpu.SMEM)
        vmem = pl.BlockSpec(memory_space=pltpu.VMEM)
        anywhere = pl.BlockSpec(memory_space=pl.ANY)
        dma = pltpu.SemaphoreType.DMA
        hidden, total = pl.pallas_call(
            functools.partial(exchange_kernel, reps, slots),
            out_shape=(
                jax.ShapeDtypeStruct((128, 256), BF16),
                jax.ShapeDtypeStruct((4, 4, 8, 128), F32),
            ),
            in_specs=[smem] * 3 + [anywhere] * 6,
            out_specs=(anywhere, anywhere),
            scratch_shapes=[
                pltpu.VMEM((64, 32, 128), BF16),
                pltpu.VMEM((32, slots, 128, 128), BF16),
                pltpu.VMEM((32, 32, 128), BF16),
                pltpu.VMEM((PLANE, 64, 128), BF16),
                pltpu.VMEM((PLANE, 64, 128), BF16),
                pltpu.VMEM((PLANE, 64, 256), BF16),
                pltpu.VMEM((PLANE, 128, 256), BF16),
                pltpu.VMEM((128, 256), BF16),
                pltpu.VMEM((1, 256), F32),
                pltpu.VMEM((128, 256), BF16),
                pltpu.VMEM((4, 4, 8, 128), F32),
                pltpu.VMEM((4, 4, 8, 128), F32),
                pltpu.VMEM((4, 4, 8, 128), F32),
                pltpu.VMEM((4, 8, 128), F32),
                dma((5,)),
                dma((8,)),
                dma((2,)),
                pltpu.SemaphoreType.REGULAR((2,)),
                dma,
                dma((PLANE,)),
                dma((PLANE,)),
                dma((PLANE,)),
                dma((2 * PLANE,)),
                dma((2 * PLANE,)),
                dma((9,)),
                dma((9,)),
            ],
            compiler_params=pltpu.CompilerParams(collective_id=0, has_side_effects=True),
            name="exchange",
        )(
            tile_src.transpose(2, 0, 1),
            tile_count,
            owner_order,
            feats[0].T,
            tile_weight[0],
            w_self,
            w_neigh,
            bias.reshape(1, -1),
            cotangent[0],
        )
        return pl.pallas_call(
            finish_kernel,
            out_shape=(
                jax.ShapeDtypeStruct((1, 128, 256), BF16),
                jax.ShapeDtypeStruct((32, 256), F32),
                jax.ShapeDtypeStruct((32, 256), F32),
            ),
            in_specs=[vmem] * 2,
            out_specs=(vmem,) * 3,
            name="finish",
        )(hidden, total)

    in_specs = (
        P("rep", None, "feat"),
        P("feat", None),
        P("feat", None),
        P(),
        P("rep", None, None, None, None),
        P("rep", None, None),
        P("rep", None),
        P("rep", None),
        P("rep", "feat", None),
    )
    out_specs = (P("rep", "feat", None), P("feat", None), P("feat", None))
    return jax.shard_map(body, mesh=mesh, in_specs=in_specs, out_specs=out_specs, check_vma=False)
```

```python
import functools

import jax
import jax.numpy as jnp
from jax import lax
from jax.experimental import pallas as pl
from jax.experimental.pallas import tpu as pltpu
from jax.sharding import PartitionSpec as P

MESH = pl.DeviceIdType.MESH
SIDE = 4
PLANE = 2 * SIDE * SIDE
F32 = jnp.float32
BF16 = jnp.bfloat16


def remote(src, dst, send_sem, recv_sem, axis, index):
    return pltpu.make_async_remote_copy(
        src_ref=src,
        dst_ref=dst,
        send_sem=send_sem,
        recv_sem=recv_sem,
        device_id={axis: index},
        device_id_type=MESH,
    )


def exchange_kernel(
    reps,
    slots,
    src_hbm,
    count_hbm,
    order_hbm,
    feats_hbm,
    tiles_hbm,
    w_self_hbm,
    w_neigh_hbm,
    bias_hbm,
    cot_hbm,
    hidden_out,
    total_out,
    src_ref,
    count_ref,
    order_ref,
    feats,
    tiles,
    means,
    mine,
    rows,
    weights,
    grads,
    cot,
    bias,
    hidden,
    part,
    near,
    far,
    whole,
    load_sems,
    tile_sems,
    out_sems,
    ready_sems,
    a2a_send,
    a2a_recv,
    w_send,
    w_recv,
    g_send,
    g_recv,
    z_send,
    z_recv,
):
    me = lax.axis_index("feat")
    z = lax.axis_index("rep")
    x, y, c = me // (2 * SIDE), (me // 2) % SIDE, me % 2
    blocks = tiles.shape[0]
    chunks = tile_sems.shape[0]
    chunk = blocks // chunks

    barrier = pltpu.get_barrier_semaphore()

    at_x = [lax.rem(x + d, SIDE) * (2 * SIDE) for d in range(SIDE)]
    at_y = [lax.rem(y + d, SIDE) * 2 for d in range(SIDE)]
    at_c = [c, 1 - c]
    at = lambda dx, dy, dc: at_x[dx % SIDE] + at_y[dy % SIDE] + at_c[dc]
    first = lambda k: (k * (1 - c) * SIDE + k * c) * 2
    second = lambda k: (k * c * SIDE + k * (1 - c)) * 2
    first_at = lambda k: at(k, 0, 0) * (1 - c) + at(0, k, 0) * c
    second_at = lambda k: at(k, 0, 0) * c + at(0, k, 0) * (1 - c)
    partner = at(0, 0, 1)
    near_first = (1, 3, 2)
    along = lambda o: lax.rem(z + reps + o, reps)

    def signal(sem, axis, index):
        pl.semaphore_signal(sem, inc=1, device_id={axis: index}, device_id_type=MESH)

    for k in near_first:
        signal(barrier, "feat", at(k, 0, 0))
        signal(barrier, "feat", at(0, k, 0))
    signal(barrier, "feat", partner)
    for o in (1, -1, 2, -2):
        signal(barrier, "rep", along(o))

    index_loads = [
        pltpu.make_async_copy(src_hbm, src_ref, load_sems.at[5]),
        pltpu.make_async_copy(count_hbm, count_ref, load_sems.at[6]),
        pltpu.make_async_copy(order_hbm, order_ref, load_sems.at[7]),
    ]
    for load in index_loads:
        load.start()
    w_loads = [
        pltpu.make_async_copy(w_self_hbm, weights.at[0, pl.ds(0, 32)], load_sems.at[0]),
        pltpu.make_async_copy(w_neigh_hbm, weights.at[0, pl.ds(32, 32)], load_sems.at[1]),
    ]
    for load in w_loads:
        load.start()

    def load_block(s, carry):
        lanes = pl.ds(pl.multiple_of(s * 128, 128), 128)
        pltpu.make_async_copy(feats_hbm.at[:, lanes], feats.at[s], load_sems.at[2]).start()
        return carry

    lax.fori_loop(0, feats.shape[0], load_block, 0)
    tile_loads = []
    for i in range(chunks):
        piece = pl.ds(i * chunk, chunk)
        tile_loads.append(pltpu.make_async_copy(tiles_hbm.at[piece], tiles.at[piece], tile_sems.at[i]))
        tile_loads[-1].start()
    small_loads = [
        pltpu.make_async_copy(bias_hbm, bias, load_sems.at[3]),
        pltpu.make_async_copy(cot_hbm, cot, load_sems.at[4]),
    ]
    for load in small_loads:
        load.start()

    class Gather:
        def __init__(self, buffer, send, recv, cuts):
            self.buffer, self.send, self.recv, self.cuts = buffer, send, recv, cuts
            self.height = buffer.shape[1] // cuts
            self.sent = []

        def ref(self, slot, h):
            return self.buffer.at[slot, pl.ds(h * self.height, self.height)]

        def go(self, source, target, h, index):
            copy = remote(
                self.ref(source, h),
                self.ref(target, h),
                self.send.at[len(self.sent)],
                self.recv.at[target * self.cuts + h],
                "feat",
                index,
            )
            copy.start()
            self.sent.append(copy)

        def got(self, slot, h):
            ref = self.ref(slot, h)
            sem = self.recv.at[slot * self.cuts + h]
            remote(ref, ref, self.send.at[0], sem, "feat", partner).wait_recv()

        def stage_one(self):
            for h in range(self.cuts):
                for k in near_first:
                    self.go(0, first(k), h, first_at(k))
            for h in range(self.cuts):
                for k in near_first:
                    self.go(0, second(k), h, second_at(k))
            for h in range(self.cuts):
                self.go(0, 1, h, partner)

        def forward(self, k, h):
            self.got(first(k), h)
            for j in near_first:
                self.go(first(k), first(k) + second(j), h, second_at(j))
            self.go(first(k), first(k) + 1, h, partner)

        def cross(self, slot, h):
            self.got(slot, h)
            self.go(slot, slot + 1, h, partner)

        def take(self, slot):
            for h in range(self.cuts):
                self.got(slot, h)

        def drain(self):
            for copy in self.sent:
                copy.wait_send()

    for load in w_loads:
        load.wait()
    pl.semaphore_wait(barrier, 11)
    w_gather = Gather(weights, w_send, w_recv, 1)
    w_gather.stage_one()
    for k in near_first:
        signal(ready_sems.at[k], "feat", first_at(k))
    signal(ready_sems.at[4], "rep", along(2))
    signal(ready_sems.at[5], "rep", along(-2))

    def pass_on():
        for i in (1, 3, 2, 4, 5):
            pl.semaphore_wait(ready_sems.at[i], 1)
        signal(ready_sems.at[0], "feat", partner)
        signal(ready_sems.at[6], "rep", along(4))
        signal(ready_sems.at[7], "rep", along(-4))

    for load in index_loads:
        load.wait()
    pltpu.make_async_copy(feats, feats, load_sems.at[2]).wait()
    for b in range(blocks):
        if b % chunk == 0:
            tile_loads[b // chunk].wait()
        if b == blocks - chunk:
            pass_on()
        used = count_ref[0, b]
        left = jnp.concatenate(
            [feats[src_ref[k, 0, b]] * (k < used).astype(F32).astype(BF16) for k in range(slots)],
            axis=1,
        )
        right = jnp.concatenate([tiles[b, k] for k in range(slots)], axis=1)
        means[b] = lax.dot_general(
            left, right, (((1,), (1,)), ((), ())), preferred_element_type=F32
        ).astype(BF16)

    def arrange(p, carry):
        block = order_ref[0, p]
        mine[p, 0:32, :] = feats[block]
        mine[p, 32:64, :] = means[block]
        return carry

    lax.fori_loop(0, PLANE, arrange, 0, unroll=4)

    pl.semaphore_wait(ready_sems.at[0], 1)
    w_gather.forward(1, 0)
    w_gather.forward(3, 0)
    for d in list(range(16, 24)) + list(range(8, 16)) + list(range(24, 32)) + list(range(1, 8)):
        target = at(d // (2 * SIDE), d // 2 % SIDE, d % 2)
        remote(
            mine.at[target], rows.at[d], a2a_send, a2a_recv.at[d], "feat", target
        ).start()
    w_gather.forward(2, 0)
    rows[0] = mine[me]
    for load in small_loads:
        load.wait()

    for k in near_first:
        w_gather.cross(second(k), 0)
    for k in near_first:
        for j in near_first:
            w_gather.cross(first(k) + second(j), 0)
    for s in range(SIDE * SIDE):
        w_gather.take(2 * s + 1)

    preact = jnp.broadcast_to(bias[...], (128, 256))
    for g in (0, 1, 2, 3, 6, 7, 4, 5):
        for d in range(4 * g, 4 * g + 4):
            if d:
                remote(
                    rows.at[d], rows.at[d], a2a_send, a2a_recv.at[d], "feat", partner
                ).wait_recv()
        left = rows[4 * g : 4 * g + 4].reshape(256, 128)
        right = weights[4 * g : 4 * g + 4].reshape(256, 256)
        preact = preact + lax.dot_general(
            left, right, (((0,), (0,)), ((), ())), preferred_element_type=F32
        )
    squash = jax.nn.sigmoid(preact)
    slope = cot[...].astype(F32) * squash * (1.0 + preact * (1.0 - squash))
    grads[0] = slope.astype(BF16)
    g_gather = Gather(grads, g_send, g_recv, 2)
    g_gather.stage_one()
    hidden[...] = (preact * squash).astype(BF16)
    hidden_copy = pltpu.make_async_copy(hidden, hidden_out, out_sems.at[0])
    hidden_copy.start()

    def owner(slot):
        dx, dy, dc = slot // (2 * SIDE), lax.rem(slot // 2, SIDE), lax.rem(slot, 2)
        return (
            lax.rem(x + SIDE - dx, SIDE) * (2 * SIDE)
            + lax.rem(y + SIDE - dy, SIDE) * 2
            + lax.rem(c + dc, 2)
        )

    def terms(group):
        result = jnp.zeros((64, 256), F32)
        for i in range(0, len(group), 2):
            pair = group[i : i + 2]
            left = jnp.concatenate([mine[owner(slot)] for slot in pair], axis=1)
            right = jnp.concatenate([grads[slot] for slot in pair], axis=0)
            result = result + jnp.dot(left, right, preferred_element_type=F32)
        return result

    corners = [(k, j) for k in near_first for j in near_first]
    for h in range(2):
        for k in near_first:
            g_gather.forward(k, h)
    for h in range(2):
        for k in near_first:
            g_gather.cross(second(k), h)
    straight = [side(k) for k in near_first for side in (first, second)]
    grad = terms([jnp.int32(0)] + straight)
    g_gather.take(1)
    for slot in straight:
        g_gather.take(slot + 1)
    grad = grad + terms([jnp.int32(1)] + [slot + 1 for slot in straight])
    for h in range(2):
        for k, j in corners:
            g_gather.cross(first(k) + second(j), h)
    grad = grad + terms([first(k) + second(j) for k, j in corners])
    last = [second(k) + first(j) + 1 for k, j in corners]
    for slot in last:
        g_gather.take(slot)
    grad = grad + terms(last)

    for row in range(8):
        for col in range(2):
            piece = row * 2 + col
            part[piece // 4, piece % 4] = grad[row * 8 : row * 8 + 8, col * 128 : col * 128 + 128]

    sent = []

    def send_rep(source, target, offset):
        copy = remote(
            source,
            target,
            z_send.at[len(sent)],
            z_recv.at[len(sent)],
            "rep",
            lax.rem(z + reps + offset, reps),
        )
        copy.start()
        sent.append(copy)

    for o in (2, 1, -1):
        send_rep(part.at[lax.rem(z + 4 + o, 4)], near.at[o % 4], o)
    for copy in sent[0:3]:
        copy.wait_recv()
    far[z // 4] = (part[lax.rem(z, 4)] + near[2]) + (near[1] + near[3])
    pl.semaphore_wait(ready_sems.at[6], 1)
    pl.semaphore_wait(ready_sems.at[7], 1)
    for o in (8, 4, -4):
        send_rep(far.at[z // 4], far.at[z // 4], o)
    for i, o in enumerate((8, 4, -4)):
        slot = far.at[lax.rem(z + reps - o, reps) // 4]
        remote(slot, slot, z_send.at[3 + i], z_recv.at[3 + i], "rep", z).wait_recv()
    whole[...] = (far[0] + far[1]) + (far[2] + far[3])
    for o in (2, 1, -1):
        send_rep(whole, total_out.at[o % 4], o)
    own = pltpu.make_async_copy(whole, total_out.at[0], out_sems.at[1])
    own.start()

    for copy in sent[0:6]:
        copy.wait_send()
    all_rows = pl.ds(1, PLANE - 1)
    remote(
        mine.at[all_rows], mine.at[all_rows], a2a_send, a2a_recv.at[0], "feat", partner
    ).wait_send()
    w_gather.drain()
    g_gather.drain()
    hidden_copy.wait()
    own.wait()
    for copy in sent[6:9]:
        copy.wait()


def finish_kernel(hidden_in, total_in, hidden_ref, grad_self_ref, grad_neigh_ref):
    z = lax.axis_index("rep")
    hidden_ref[0] = hidden_in[...]
    for piece in range(16):
        row, col = piece // 2, piece % 2
        value = total_in[lax.rem(z + 4 - piece // 4, 4), piece % 4]
        target = grad_self_ref if row < 4 else grad_neigh_ref
        target[row % 4 * 8 : row % 4 * 8 + 8, col * 128 : col * 128 + 128] = value


def solution(mesh):
    reps = mesh.shape["rep"]

    def body(feats, w_self, w_neigh, bias, tile_weight, tile_src, tile_count, owner_order, cotangent):
        slots = tile_weight.shape[2]
        vmem = pl.BlockSpec(memory_space=pltpu.VMEM)
        anywhere = pl.BlockSpec(memory_space=pl.ANY)
        dma = pltpu.SemaphoreType.DMA
        hidden, total = pl.pallas_call(
            functools.partial(exchange_kernel, reps, slots),
            out_shape=(
                jax.ShapeDtypeStruct((128, 256), BF16),
                jax.ShapeDtypeStruct((4, 4, 8, 128), F32),
            ),
            in_specs=[anywhere] * 9,
            out_specs=(anywhere, anywhere),
            scratch_shapes=[
                pltpu.SMEM((slots, 1, 32), jnp.int32),
                pltpu.SMEM((1, 32), jnp.int32),
                pltpu.SMEM((1, 32), jnp.int32),
                pltpu.VMEM((64, 32, 128), BF16),
                pltpu.VMEM((32, slots, 128, 128), BF16),
                pltpu.VMEM((32, 32, 128), BF16),
                pltpu.VMEM((PLANE, 64, 128), BF16),
                pltpu.VMEM((PLANE, 64, 128), BF16),
                pltpu.VMEM((PLANE, 64, 256), BF16),
                pltpu.VMEM((PLANE, 128, 256), BF16),
                pltpu.VMEM((128, 256), BF16),
                pltpu.VMEM((1, 256), F32),
                pltpu.VMEM((128, 256), BF16),
                pltpu.VMEM((4, 4, 8, 128), F32),
                pltpu.VMEM((4, 4, 8, 128), F32),
                pltpu.VMEM((4, 4, 8, 128), F32),
                pltpu.VMEM((4, 8, 128), F32),
                dma((8,)),
                dma((8,)),
                dma((2,)),
                pltpu.SemaphoreType.REGULAR((8,)),
                dma,
                dma((PLANE,)),
                dma((PLANE,)),
                dma((PLANE,)),
                dma((2 * PLANE,)),
                dma((2 * PLANE,)),
                dma((9,)),
                dma((9,)),
            ],
            compiler_params=pltpu.CompilerParams(collective_id=0, has_side_effects=True),
            name="exchange",
        )(
            tile_src.transpose(2, 0, 1),
            tile_count,
            owner_order,
            feats[0].T,
            tile_weight[0],
            w_self,
            w_neigh,
            bias.reshape(1, -1),
            cotangent[0],
        )
        return pl.pallas_call(
            finish_kernel,
            out_shape=(
                jax.ShapeDtypeStruct((1, 128, 256), BF16),
                jax.ShapeDtypeStruct((32, 256), F32),
                jax.ShapeDtypeStruct((32, 256), F32),
            ),
            in_specs=[vmem] * 2,
            out_specs=(vmem,) * 3,
            name="finish",
        )(hidden, total)

    in_specs = (
        P("rep", None, "feat"),
        P("feat", None),
        P("feat", None),
        P(),
        P("rep", None, None, None, None),
        P("rep", None, None),
        P("rep", None),
        P("rep", None),
        P("rep", "feat", None),
    )
    out_specs = (P("rep", "feat", None), P("feat", None), P("feat", None))
    return jax.shard_map(body, mesh=mesh, in_specs=in_specs, out_specs=out_specs, check_vma=False)
```

```python
import functools

import jax
import jax.numpy as jnp
from jax import lax
from jax.experimental import pallas as pl
from jax.experimental.pallas import tpu as pltpu
from jax.sharding import PartitionSpec as P

MESH = pl.DeviceIdType.MESH
SIDE = 4
PLANE = 2 * SIDE * SIDE
F32 = jnp.float32
BF16 = jnp.bfloat16


def remote(src, dst, send_sem, recv_sem, axis, index):
    return pltpu.make_async_remote_copy(
        src_ref=src,
        dst_ref=dst,
        send_sem=send_sem,
        recv_sem=recv_sem,
        device_id={axis: index},
        device_id_type=MESH,
    )


def exchange_kernel(
    reps,
    slots,
    src_hbm,
    count_hbm,
    order_hbm,
    feats_hbm,
    tiles_hbm,
    w_self_hbm,
    w_neigh_hbm,
    bias_hbm,
    cot_hbm,
    hidden_out,
    total_out,
    src_ref,
    count_ref,
    order_ref,
    feats,
    tiles,
    means,
    mine,
    rows,
    weights,
    grads,
    cot,
    bias,
    hidden,
    part,
    near,
    far,
    whole,
    load_sems,
    feat_sems,
    tile_sems,
    out_sems,
    ready_sems,
    a2a_send,
    a2a_recv,
    w_send,
    w_recv,
    g_send,
    g_recv,
    z_send,
    z_recv,
):
    me = lax.axis_index("feat")
    z = lax.axis_index("rep")
    x, y, c = me // (2 * SIDE), (me // 2) % SIDE, me % 2
    blocks = tiles.shape[0]
    chunks = tile_sems.shape[0]
    chunk = blocks // chunks

    barrier = pltpu.get_barrier_semaphore()

    at_x = [lax.rem(x + d, SIDE) * (2 * SIDE) for d in range(SIDE)]
    at_y = [lax.rem(y + d, SIDE) * 2 for d in range(SIDE)]
    at_c = [c, 1 - c]
    at = lambda dx, dy, dc: at_x[dx % SIDE] + at_y[dy % SIDE] + at_c[dc]
    first = lambda k: (k * (1 - c) * SIDE + k * c) * 2
    second = lambda k: (k * c * SIDE + k * (1 - c)) * 2
    first_at = lambda k: at(k, 0, 0) * (1 - c) + at(0, k, 0) * c
    second_at = lambda k: at(k, 0, 0) * c + at(0, k, 0) * (1 - c)
    partner = at(0, 0, 1)
    near_first = (1, 3, 2)
    along = lambda o: lax.rem(z + reps + o, reps)

    def signal(sem, axis, index):
        pl.semaphore_signal(sem, inc=1, device_id={axis: index}, device_id_type=MESH)

    for k in near_first:
        signal(barrier, "feat", at(k, 0, 0))
        signal(barrier, "feat", at(0, k, 0))
    signal(barrier, "feat", partner)
    for o in (1, -1, 2, -2):
        signal(barrier, "rep", along(o))

    index_loads = [
        pltpu.make_async_copy(src_hbm, src_ref, load_sems.at[5]),
        pltpu.make_async_copy(count_hbm, count_ref, load_sems.at[6]),
        pltpu.make_async_copy(order_hbm, order_ref, load_sems.at[7]),
    ]
    w_loads = [
        pltpu.make_async_copy(w_self_hbm, weights.at[0, pl.ds(0, 32)], load_sems.at[0]),
        pltpu.make_async_copy(w_neigh_hbm, weights.at[0, pl.ds(32, 32)], load_sems.at[1]),
    ]
    feat_loads = [
        pltpu.make_async_copy(
            feats_hbm.at[i], feats.at[:, pl.ds(i * 8, 8)], feat_sems.at[i]
        )
        for i in range(4)
    ]
    small_loads = [
        pltpu.make_async_copy(bias_hbm, bias, load_sems.at[3]),
        pltpu.make_async_copy(cot_hbm, cot, load_sems.at[4]),
    ]

    def tile_load(i):
        piece = pl.ds(i * chunk, chunk)
        return pltpu.make_async_copy(tiles_hbm.at[piece], tiles.at[piece], tile_sems.at[i])

    for load in w_loads + index_loads:
        load.start()
    tile_load(0).start()
    for load in feat_loads:
        load.start()
    for i in range(1, chunks):
        tile_load(i).start()
    for load in small_loads:
        load.start()

    class Gather:
        def __init__(self, buffer, send, recv, cuts):
            self.buffer, self.send, self.recv, self.cuts = buffer, send, recv, cuts
            self.height = buffer.shape[1] // cuts
            self.sent = []

        def ref(self, slot, h):
            return self.buffer.at[slot, pl.ds(h * self.height, self.height)]

        def go(self, source, target, h, index):
            copy = remote(
                self.ref(source, h),
                self.ref(target, h),
                self.send.at[len(self.sent)],
                self.recv.at[target * self.cuts + h],
                "feat",
                index,
            )
            copy.start()
            self.sent.append(copy)

        def got(self, slot, h):
            ref = self.ref(slot, h)
            sem = self.recv.at[slot * self.cuts + h]
            remote(ref, ref, self.send.at[0], sem, "feat", partner).wait_recv()

        def stage_one(self):
            for h in range(self.cuts):
                for k in near_first:
                    self.go(0, first(k), h, first_at(k))
            for h in range(self.cuts):
                for k in near_first:
                    self.go(0, second(k), h, second_at(k))
            for h in range(self.cuts):
                self.go(0, 1, h, partner)

        def forward(self, k, h):
            self.got(first(k), h)
            for j in near_first:
                self.go(first(k), first(k) + second(j), h, second_at(j))
            self.go(first(k), first(k) + 1, h, partner)

        def cross(self, slot, h):
            self.got(slot, h)
            self.go(slot, slot + 1, h, partner)

        def take(self, slot):
            for h in range(self.cuts):
                self.got(slot, h)

        def drain(self):
            for copy in self.sent:
                copy.wait_send()

    for load in w_loads:
        load.wait()
    pl.semaphore_wait(barrier, 11)
    w_gather = Gather(weights, w_send, w_recv, 1)
    w_gather.stage_one()
    for k in near_first:
        signal(ready_sems.at[k], "feat", first_at(k))
    signal(ready_sems.at[4], "rep", along(2))
    signal(ready_sems.at[5], "rep", along(-2))

    for load in index_loads + feat_loads:
        load.wait()

    def combine(i, carry):
        tile_load(i).wait()
        for b in range(chunk):
            block = i * chunk + b
            used = count_ref[0, block]
            left = jnp.concatenate(
                [
                    feats[src_ref[k, 0, block]] * (k < used).astype(F32).astype(BF16)
                    for k in range(slots)
                ],
                axis=1,
            )
            right = jnp.concatenate([tiles[block, k] for k in range(slots)], axis=1)
            means[block] = lax.dot_general(
                left, right, (((1,), (1,)), ((), ())), preferred_element_type=F32
            ).astype(BF16)
        return carry

    lax.fori_loop(0, chunks - 1, combine, 0)
    for k in near_first:
        pl.semaphore_wait(ready_sems.at[k], 1)
    signal(ready_sems.at[0], "feat", partner)
    for k in near_first:
        w_gather.forward(k, 0)
    lax.fori_loop(chunks - 1, chunks, combine, 0)

    def arrange(p, carry):
        block = order_ref[0, p]
        mine[p, 0:32, :] = feats[block]
        mine[p, 32:64, :] = means[block]
        return carry

    lax.fori_loop(0, PLANE, arrange, 0, unroll=4)

    pl.semaphore_wait(ready_sems.at[0], 1)
    for d in list(range(16, 24)) + list(range(8, 16)) + list(range(24, 32)) + list(range(1, 8)):
        target = at(d // (2 * SIDE), d // 2 % SIDE, d % 2)
        remote(
            mine.at[target], rows.at[d], a2a_send, a2a_recv.at[d], "feat", target
        ).start()
    for i in (4, 5):
        pl.semaphore_wait(ready_sems.at[i], 1)
    signal(ready_sems.at[6], "rep", along(4))
    signal(ready_sems.at[7], "rep", along(-4))
    rows[0] = mine[me]
    for load in small_loads:
        load.wait()

    for k in near_first:
        w_gather.cross(second(k), 0)
    for k in near_first:
        for j in near_first:
            w_gather.cross(first(k) + second(j), 0)
    for s in range(SIDE * SIDE):
        w_gather.take(2 * s + 1)

    preact = jnp.broadcast_to(bias[...], (128, 256))
    for g in (0, 1, 2, 3, 6, 7, 4, 5):
        for d in range(4 * g, 4 * g + 4):
            if d:
                remote(
                    rows.at[d], rows.at[d], a2a_send, a2a_recv.at[d], "feat", partner
                ).wait_recv()
        left = rows[4 * g : 4 * g + 4].reshape(256, 128)
        right = weights[4 * g : 4 * g + 4].reshape(256, 256)
        preact = preact + lax.dot_general(
            left, right, (((0,), (0,)), ((), ())), preferred_element_type=F32
        )
    squash = jax.nn.sigmoid(preact)
    slope = cot[...].astype(F32) * squash * (1.0 + preact * (1.0 - squash))
    grads[0] = slope.astype(BF16)
    g_gather = Gather(grads, g_send, g_recv, 2)
    g_gather.stage_one()
    hidden[...] = (preact * squash).astype(BF16)
    hidden_copy = pltpu.make_async_copy(hidden, hidden_out, out_sems.at[0])
    hidden_copy.start()

    def owner(slot):
        dx, dy, dc = slot // (2 * SIDE), lax.rem(slot // 2, SIDE), lax.rem(slot, 2)
        return (
            lax.rem(x + SIDE - dx, SIDE) * (2 * SIDE)
            + lax.rem(y + SIDE - dy, SIDE) * 2
            + lax.rem(c + dc, 2)
        )

    def terms(group):
        result = jnp.zeros((64, 256), F32)
        for i in range(0, len(group), 2):
            pair = group[i : i + 2]
            left = jnp.concatenate([mine[owner(slot)] for slot in pair], axis=1)
            right = jnp.concatenate([grads[slot] for slot in pair], axis=0)
            result = result + jnp.dot(left, right, preferred_element_type=F32)
        return result

    corners = [(k, j) for k in near_first for j in near_first]
    for h in range(2):
        for k in near_first:
            g_gather.forward(k, h)
    for h in range(2):
        for k in near_first:
            g_gather.cross(second(k), h)
    straight = [side(k) for k in near_first for side in (first, second)]
    grad = terms([jnp.int32(0)] + straight)
    g_gather.take(1)
    for slot in straight:
        g_gather.take(slot + 1)
    grad = grad + terms([jnp.int32(1)] + [slot + 1 for slot in straight])
    for h in range(2):
        for k, j in corners:
            g_gather.cross(first(k) + second(j), h)
    grad = grad + terms([first(k) + second(j) for k, j in corners])
    last = [second(k) + first(j) + 1 for k, j in corners]
    for slot in last:
        g_gather.take(slot)
    grad = grad + terms(last)

    for row in range(8):
        for col in range(2):
            piece = row * 2 + col
            part[piece // 4, piece % 4] = grad[row * 8 : row * 8 + 8, col * 128 : col * 128 + 128]

    sent = []

    def send_rep(source, target, offset):
        copy = remote(
            source,
            target,
            z_send.at[len(sent)],
            z_recv.at[len(sent)],
            "rep",
            lax.rem(z + reps + offset, reps),
        )
        copy.start()
        sent.append(copy)

    for o in (2, 1, -1):
        send_rep(part.at[lax.rem(z + 4 + o, 4)], near.at[o % 4], o)
    for copy in sent[0:3]:
        copy.wait_recv()
    far[z // 4] = (part[lax.rem(z, 4)] + near[2]) + (near[1] + near[3])
    pl.semaphore_wait(ready_sems.at[6], 1)
    pl.semaphore_wait(ready_sems.at[7], 1)
    for o in (8, 4, -4):
        send_rep(far.at[z // 4], far.at[z // 4], o)
    for i, o in enumerate((8, 4, -4)):
        slot = far.at[lax.rem(z + reps - o, reps) // 4]
        remote(slot, slot, z_send.at[3 + i], z_recv.at[3 + i], "rep", z).wait_recv()
    whole[...] = (far[0] + far[1]) + (far[2] + far[3])
    for o in (2, 1, -1):
        send_rep(whole, total_out.at[o % 4], o)
    own = pltpu.make_async_copy(whole, total_out.at[0], out_sems.at[1])
    own.start()

    for copy in sent[0:6]:
        copy.wait_send()
    all_rows = pl.ds(1, PLANE - 1)
    remote(
        mine.at[all_rows], mine.at[all_rows], a2a_send, a2a_recv.at[0], "feat", partner
    ).wait_send()
    w_gather.drain()
    g_gather.drain()
    hidden_copy.wait()
    own.wait()
    for copy in sent[6:9]:
        copy.wait()


def finish_kernel(hidden_in, total_in, hidden_ref, grad_self_ref, grad_neigh_ref):
    z = lax.axis_index("rep")
    hidden_ref[0] = hidden_in[...]
    for piece in range(16):
        row, col = piece // 2, piece % 2
        value = total_in[lax.rem(z + 4 - piece // 4, 4), piece % 4]
        target = grad_self_ref if row < 4 else grad_neigh_ref
        target[row % 4 * 8 : row % 4 * 8 + 8, col * 128 : col * 128 + 128] = value


def solution(mesh):
    reps = mesh.shape["rep"]

    def body(feats, w_self, w_neigh, bias, tile_weight, tile_src, tile_count, owner_order, cotangent):
        slots = tile_weight.shape[2]
        vmem = pl.BlockSpec(memory_space=pltpu.VMEM)
        anywhere = pl.BlockSpec(memory_space=pl.ANY)
        dma = pltpu.SemaphoreType.DMA
        hidden, total = pl.pallas_call(
            functools.partial(exchange_kernel, reps, slots),
            out_shape=(
                jax.ShapeDtypeStruct((128, 256), BF16),
                jax.ShapeDtypeStruct((4, 4, 8, 128), F32),
            ),
            in_specs=[anywhere] * 9,
            out_specs=(anywhere, anywhere),
            scratch_shapes=[
                pltpu.SMEM((slots, 1, 32), jnp.int32),
                pltpu.SMEM((1, 32), jnp.int32),
                pltpu.SMEM((1, 32), jnp.int32),
                pltpu.VMEM((64, 32, 128), BF16),
                pltpu.VMEM((32, slots, 128, 128), BF16),
                pltpu.VMEM((32, 32, 128), BF16),
                pltpu.VMEM((PLANE, 64, 128), BF16),
                pltpu.VMEM((PLANE, 64, 128), BF16),
                pltpu.VMEM((PLANE, 64, 256), BF16),
                pltpu.VMEM((PLANE, 128, 256), BF16),
                pltpu.VMEM((128, 256), BF16),
                pltpu.VMEM((1, 256), F32),
                pltpu.VMEM((128, 256), BF16),
                pltpu.VMEM((4, 4, 8, 128), F32),
                pltpu.VMEM((4, 4, 8, 128), F32),
                pltpu.VMEM((4, 4, 8, 128), F32),
                pltpu.VMEM((4, 8, 128), F32),
                dma((8,)),
                dma((4,)),
                dma((8,)),
                dma((2,)),
                pltpu.SemaphoreType.REGULAR((8,)),
                dma,
                dma((PLANE,)),
                dma((PLANE,)),
                dma((PLANE,)),
                dma((2 * PLANE,)),
                dma((2 * PLANE,)),
                dma((9,)),
                dma((9,)),
            ],
            compiler_params=pltpu.CompilerParams(collective_id=0, has_side_effects=True),
            name="exchange",
        )(
            tile_src.transpose(2, 0, 1),
            tile_count,
            owner_order,
            feats[0].T.reshape(4, 8, 64, 128).transpose(0, 2, 1, 3),
            tile_weight[0],
            w_self,
            w_neigh,
            bias.reshape(1, -1),
            cotangent[0],
        )
        return pl.pallas_call(
            finish_kernel,
            out_shape=(
                jax.ShapeDtypeStruct((1, 128, 256), BF16),
                jax.ShapeDtypeStruct((32, 256), F32),
                jax.ShapeDtypeStruct((32, 256), F32),
            ),
            in_specs=[vmem] * 2,
            out_specs=(vmem,) * 3,
            name="finish",
        )(hidden, total)

    in_specs = (
        P("rep", None, "feat"),
        P("feat", None),
        P("feat", None),
        P(),
        P("rep", None, None, None, None),
        P("rep", None, None),
        P("rep", None),
        P("rep", None),
        P("rep", "feat", None),
    )
    out_specs = (P("rep", "feat", None), P("feat", None), P("feat", None))
    return jax.shard_map(body, mesh=mesh, in_specs=in_specs, out_specs=out_specs, check_vma=False)
```

```python
import functools

import jax
import jax.numpy as jnp
from jax import lax
from jax.experimental import pallas as pl
from jax.experimental.pallas import tpu as pltpu
from jax.sharding import PartitionSpec as P

MESH = pl.DeviceIdType.MESH
SIDE = 4
PLANE = 2 * SIDE * SIDE
F32 = jnp.float32
BF16 = jnp.bfloat16


def remote(src, dst, send_sem, recv_sem, axis, index):
    return pltpu.make_async_remote_copy(
        src_ref=src,
        dst_ref=dst,
        send_sem=send_sem,
        recv_sem=recv_sem,
        device_id={axis: index},
        device_id_type=MESH,
    )


def exchange_kernel(
    reps,
    slots,
    src_hbm,
    count_hbm,
    order_hbm,
    feats_hbm,
    tiles_hbm,
    w_self_hbm,
    w_neigh_hbm,
    bias_hbm,
    cot_hbm,
    hidden_out,
    total_out,
    src_ref,
    count_ref,
    order_ref,
    feats,
    tiles,
    means,
    mine,
    rows,
    weights,
    grads,
    cot,
    bias,
    hidden,
    part,
    near,
    far,
    whole,
    load_sems,
    feat_sems,
    tile_sems,
    out_sems,
    ready_sems,
    a2a_send,
    a2a_recv,
    w_send,
    w_recv,
    g_send,
    g_recv,
    z_send,
    z_recv,
):
    me = lax.axis_index("feat")
    z = lax.axis_index("rep")
    x, y, c = me // (2 * SIDE), (me // 2) % SIDE, me % 2
    blocks = tiles.shape[0]
    chunks = tile_sems.shape[0]
    chunk = blocks // chunks

    barrier = pltpu.get_barrier_semaphore()

    at_x = [lax.rem(x + d, SIDE) * (2 * SIDE) for d in range(SIDE)]
    at_y = [lax.rem(y + d, SIDE) * 2 for d in range(SIDE)]
    at_c = [c, 1 - c]
    at = lambda dx, dy, dc: at_x[dx % SIDE] + at_y[dy % SIDE] + at_c[dc]
    first = lambda k: (k * (1 - c) * SIDE + k * c) * 2
    second = lambda k: (k * c * SIDE + k * (1 - c)) * 2
    first_at = lambda k: at(k, 0, 0) * (1 - c) + at(0, k, 0) * c
    second_at = lambda k: at(k, 0, 0) * c + at(0, k, 0) * (1 - c)
    partner = at(0, 0, 1)
    near_first = (1, 3, 2)
    along = lambda o: lax.rem(z + reps + o, reps)

    def signal(sem, axis, index):
        pl.semaphore_signal(sem, inc=1, device_id={axis: index}, device_id_type=MESH)

    for k in near_first:
        signal(barrier, "feat", at(k, 0, 0))
        signal(barrier, "feat", at(0, k, 0))
    signal(barrier, "feat", partner)
    for o in (1, -1, 2, -2):
        signal(barrier, "rep", along(o))

    index_loads = [
        pltpu.make_async_copy(src_hbm, src_ref, load_sems.at[5]),
        pltpu.make_async_copy(count_hbm, count_ref, load_sems.at[6]),
        pltpu.make_async_copy(order_hbm, order_ref, load_sems.at[7]),
    ]
    w_loads = [
        pltpu.make_async_copy(w_self_hbm, weights.at[0, pl.ds(0, 32)], load_sems.at[0]),
        pltpu.make_async_copy(w_neigh_hbm, weights.at[0, pl.ds(32, 32)], load_sems.at[1]),
    ]
    feat_loads = [
        pltpu.make_async_copy(
            feats_hbm.at[i], feats.at[:, pl.ds(i * 8, 8)], feat_sems.at[i]
        )
        for i in range(4)
    ]
    small_loads = [
        pltpu.make_async_copy(bias_hbm, bias, load_sems.at[3]),
        pltpu.make_async_copy(cot_hbm, cot, load_sems.at[4]),
    ]

    def tile_load(i):
        piece = pl.ds(i * chunk, chunk)
        return pltpu.make_async_copy(tiles_hbm.at[piece], tiles.at[piece], tile_sems.at[i])

    for load in w_loads + index_loads:
        load.start()
    tile_load(0).start()
    for load in feat_loads:
        load.start()
    for i in range(1, chunks):
        tile_load(i).start()
    for load in small_loads:
        load.start()

    class Gather:
        def __init__(self, buffer, send, recv, cuts):
            self.buffer, self.send, self.recv, self.cuts = buffer, send, recv, cuts
            self.height = buffer.shape[1] // cuts
            self.sent = []

        def ref(self, slot, h):
            return self.buffer.at[slot, pl.ds(h * self.height, self.height)]

        def go(self, source, target, h, index):
            copy = remote(
                self.ref(source, h),
                self.ref(target, h),
                self.send.at[len(self.sent)],
                self.recv.at[target * self.cuts + h],
                "feat",
                index,
            )
            copy.start()
            self.sent.append(copy)

        def got(self, slot, h):
            ref = self.ref(slot, h)
            sem = self.recv.at[slot * self.cuts + h]
            remote(ref, ref, self.send.at[0], sem, "feat", partner).wait_recv()

        def stage_one(self):
            for h in range(self.cuts):
                for k in near_first:
                    self.go(0, first(k), h, first_at(k))
            for h in range(self.cuts):
                for k in near_first:
                    self.go(0, second(k), h, second_at(k))
            for h in range(self.cuts):
                self.go(0, 1, h, partner)

        def forward(self, k, h):
            self.got(first(k), h)
            for j in near_first:
                self.go(first(k), first(k) + second(j), h, second_at(j))
            self.go(first(k), first(k) + 1, h, partner)

        def cross(self, slot, h):
            self.got(slot, h)
            self.go(slot, slot + 1, h, partner)

        def take(self, slot):
            for h in range(self.cuts):
                self.got(slot, h)

        def drain(self):
            for copy in self.sent:
                copy.wait_send()

    for load in w_loads:
        load.wait()
    pl.semaphore_wait(barrier, 11)
    w_gather = Gather(weights, w_send, w_recv, 1)
    w_gather.stage_one()
    for k in near_first:
        signal(ready_sems.at[k], "feat", first_at(k))
    signal(ready_sems.at[4], "rep", along(2))
    signal(ready_sems.at[5], "rep", along(-2))

    for load in index_loads + feat_loads:
        load.wait()

    def combine(i, carry):
        tile_load(i).wait()
        for b in range(chunk):
            block = i * chunk + b
            used = count_ref[0, block]
            left = jnp.concatenate(
                [
                    feats[src_ref[k, 0, block]] * (k < used).astype(F32).astype(BF16)
                    for k in range(slots)
                ],
                axis=1,
            )
            right = jnp.concatenate([tiles[block, k] for k in range(slots)], axis=1)
            means[block] = lax.dot_general(
                left, right, (((1,), (1,)), ((), ())), preferred_element_type=F32
            ).astype(BF16)
        return carry

    peers = [
        (dx, dy, dc)
        for dy, dc in ((2, 0), (1, 1), (3, 0), (0, 1), (2, 1), (1, 0), (3, 1), (0, 0))
        for dx in (2, 1, 3, 0)
        if (dx, dy, dc) != (0, 0, 0)
    ]

    def row_copy(part, source, d, target):
        half = pl.ds(part * 32, 32)
        return remote(
            mine.at[source, half],
            rows.at[d, half],
            a2a_send.at[part],
            a2a_recv.at[part, d],
            "feat",
            target,
        )

    def send_rows(part):
        for dx, dy, dc in peers:
            target = at(dx, dy, dc)
            row_copy(part, target, (dx * SIDE + dy) * 2 + dc, target).start()

    def arrange_rows(p, carry):
        mine[p, 0:32, :] = feats[order_ref[0, p]]
        return carry

    def arrange_means(p, carry):
        mine[p, 32:64, :] = means[order_ref[0, p]]
        return carry

    lax.fori_loop(0, PLANE, arrange_rows, 0, unroll=8)
    lax.fori_loop(0, 4, combine, 0)
    for k in near_first:
        pl.semaphore_wait(ready_sems.at[k], 1)
    signal(ready_sems.at[0], "feat", partner)
    lax.fori_loop(4, 6, combine, 0)
    pl.semaphore_wait(ready_sems.at[0], 1)
    send_rows(0)
    lax.fori_loop(6, chunks, combine, 0)
    lax.fori_loop(0, PLANE, arrange_means, 0, unroll=8)
    for k in near_first:
        w_gather.forward(k, 0)
    send_rows(1)
    for i in (4, 5):
        pl.semaphore_wait(ready_sems.at[i], 1)
    signal(ready_sems.at[6], "rep", along(4))
    signal(ready_sems.at[7], "rep", along(-4))
    rows[0] = mine[me]
    for load in small_loads:
        load.wait()

    for k in near_first:
        w_gather.cross(second(k), 0)
    for k in near_first:
        for j in near_first:
            w_gather.cross(first(k) + second(j), 0)
    for s in range(SIDE * SIDE):
        w_gather.take(2 * s + 1)

    preact = jnp.broadcast_to(bias[...], (128, 256))
    for g in (0, 1, 2, 3, 6, 7, 4, 5):
        for d in range(4 * g, 4 * g + 4):
            if d:
                row_copy(0, 0, d, partner).wait_recv()
                row_copy(1, 0, d, partner).wait_recv()
        left = rows[4 * g : 4 * g + 4].reshape(256, 128)
        right = weights[4 * g : 4 * g + 4].reshape(256, 256)
        preact = preact + lax.dot_general(
            left, right, (((0,), (0,)), ((), ())), preferred_element_type=F32
        )
    squash = jax.nn.sigmoid(preact)
    slope = cot[...].astype(F32) * squash * (1.0 + preact * (1.0 - squash))
    grads[0] = slope.astype(BF16)
    g_gather = Gather(grads, g_send, g_recv, 2)
    g_gather.stage_one()
    hidden[...] = (preact * squash).astype(BF16)
    hidden_copy = pltpu.make_async_copy(hidden, hidden_out, out_sems.at[0])
    hidden_copy.start()

    def owner(slot):
        dx, dy, dc = slot // (2 * SIDE), lax.rem(slot // 2, SIDE), lax.rem(slot, 2)
        return (
            lax.rem(x + SIDE - dx, SIDE) * (2 * SIDE)
            + lax.rem(y + SIDE - dy, SIDE) * 2
            + lax.rem(c + dc, 2)
        )

    def terms(group):
        result = jnp.zeros((64, 256), F32)
        for i in range(0, len(group), 2):
            pair = group[i : i + 2]
            left = jnp.concatenate([mine[owner(slot)] for slot in pair], axis=1)
            right = jnp.concatenate([grads[slot] for slot in pair], axis=0)
            result = result + jnp.dot(left, right, preferred_element_type=F32)
        return result

    corners = [(k, j) for k in near_first for j in near_first]
    for h in range(2):
        for k in near_first:
            g_gather.forward(k, h)
    for h in range(2):
        for k in near_first:
            g_gather.cross(second(k), h)
    straight = [side(k) for k in near_first for side in (first, second)]
    grad = terms([jnp.int32(0)] + straight)
    g_gather.take(1)
    for slot in straight:
        g_gather.take(slot + 1)
    grad = grad + terms([jnp.int32(1)] + [slot + 1 for slot in straight])
    for h in range(2):
        for k, j in corners:
            g_gather.cross(first(k) + second(j), h)
    grad = grad + terms([first(k) + second(j) for k, j in corners])
    last = [second(k) + first(j) + 1 for k, j in corners]
    for slot in last:
        g_gather.take(slot)
    grad = grad + terms(last)

    for row in range(8):
        for col in range(2):
            piece = row * 2 + col
            part[piece // 4, piece % 4] = grad[row * 8 : row * 8 + 8, col * 128 : col * 128 + 128]

    sent = []

    def send_rep(source, target, offset):
        copy = remote(
            source,
            target,
            z_send.at[len(sent)],
            z_recv.at[len(sent)],
            "rep",
            lax.rem(z + reps + offset, reps),
        )
        copy.start()
        sent.append(copy)

    for o in (2, 1, -1):
        send_rep(part.at[lax.rem(z + 4 + o, 4)], near.at[o % 4], o)
    for copy in sent[0:3]:
        copy.wait_recv()
    far[z // 4] = (part[lax.rem(z, 4)] + near[2]) + (near[1] + near[3])
    pl.semaphore_wait(ready_sems.at[6], 1)
    pl.semaphore_wait(ready_sems.at[7], 1)
    for o in (8, 4, -4):
        send_rep(far.at[z // 4], far.at[z // 4], o)
    for i, o in enumerate((8, 4, -4)):
        slot = far.at[lax.rem(z + reps - o, reps) // 4]
        remote(slot, slot, z_send.at[3 + i], z_recv.at[3 + i], "rep", z).wait_recv()
    whole[...] = (far[0] + far[1]) + (far[2] + far[3])
    for o in (2, 1, -1):
        send_rep(whole, total_out.at[o % 4], o)
    own = pltpu.make_async_copy(whole, total_out.at[0], out_sems.at[1])
    own.start()

    for copy in sent[0:6]:
        copy.wait_send()
    for part in range(2):
        sent_rows = mine.at[pl.ds(1, PLANE - 1), pl.ds(part * 32, 32)]
        remote(
            sent_rows, sent_rows, a2a_send.at[part], a2a_recv.at[part, 0], "feat", partner
        ).wait_send()
    w_gather.drain()
    g_gather.drain()
    hidden_copy.wait()
    own.wait()
    for copy in sent[6:9]:
        copy.wait()


def finish_kernel(hidden_in, total_in, hidden_ref, grad_self_ref, grad_neigh_ref):
    z = lax.axis_index("rep")
    hidden_ref[0] = hidden_in[...]
    for piece in range(16):
        row, col = piece // 2, piece % 2
        value = total_in[lax.rem(z + 4 - piece // 4, 4), piece % 4]
        target = grad_self_ref if row < 4 else grad_neigh_ref
        target[row % 4 * 8 : row % 4 * 8 + 8, col * 128 : col * 128 + 128] = value


def solution(mesh):
    reps = mesh.shape["rep"]

    def body(feats, w_self, w_neigh, bias, tile_weight, tile_src, tile_count, owner_order, cotangent):
        slots = tile_weight.shape[2]
        vmem = pl.BlockSpec(memory_space=pltpu.VMEM)
        anywhere = pl.BlockSpec(memory_space=pl.ANY)
        dma = pltpu.SemaphoreType.DMA
        hidden, total = pl.pallas_call(
            functools.partial(exchange_kernel, reps, slots),
            out_shape=(
                jax.ShapeDtypeStruct((128, 256), BF16),
                jax.ShapeDtypeStruct((4, 4, 8, 128), F32),
            ),
            in_specs=[anywhere] * 9,
            out_specs=(anywhere, anywhere),
            scratch_shapes=[
                pltpu.SMEM((slots, 1, 32), jnp.int32),
                pltpu.SMEM((1, 32), jnp.int32),
                pltpu.SMEM((1, 32), jnp.int32),
                pltpu.VMEM((64, 32, 128), BF16),
                pltpu.VMEM((32, slots, 128, 128), BF16),
                pltpu.VMEM((32, 32, 128), BF16),
                pltpu.VMEM((PLANE, 64, 128), BF16),
                pltpu.VMEM((PLANE, 64, 128), BF16),
                pltpu.VMEM((PLANE, 64, 256), BF16),
                pltpu.VMEM((PLANE, 128, 256), BF16),
                pltpu.VMEM((128, 256), BF16),
                pltpu.VMEM((1, 256), F32),
                pltpu.VMEM((128, 256), BF16),
                pltpu.VMEM((4, 4, 8, 128), F32),
                pltpu.VMEM((4, 4, 8, 128), F32),
                pltpu.VMEM((4, 4, 8, 128), F32),
                pltpu.VMEM((4, 8, 128), F32),
                dma((8,)),
                dma((4,)),
                dma((8,)),
                dma((2,)),
                pltpu.SemaphoreType.REGULAR((8,)),
                dma((2,)),
                dma((2, PLANE)),
                dma((PLANE,)),
                dma((PLANE,)),
                dma((2 * PLANE,)),
                dma((2 * PLANE,)),
                dma((9,)),
                dma((9,)),
            ],
            compiler_params=pltpu.CompilerParams(collective_id=0, has_side_effects=True),
            name="exchange",
        )(
            tile_src.transpose(2, 0, 1),
            tile_count,
            owner_order,
            feats[0].T.reshape(4, 8, 64, 128).transpose(0, 2, 1, 3),
            tile_weight[0],
            w_self,
            w_neigh,
            bias.reshape(1, -1),
            cotangent[0],
        )
        return pl.pallas_call(
            finish_kernel,
            out_shape=(
                jax.ShapeDtypeStruct((1, 128, 256), BF16),
                jax.ShapeDtypeStruct((32, 256), F32),
                jax.ShapeDtypeStruct((32, 256), F32),
            ),
            in_specs=[vmem] * 2,
            out_specs=(vmem,) * 3,
            name="finish",
        )(hidden, total)

    in_specs = (
        P("rep", None, "feat"),
        P("feat", None),
        P("feat", None),
        P(),
        P("rep", None, None, None, None),
        P("rep", None, None),
        P("rep", None),
        P("rep", None),
        P("rep", "feat", None),
    )
    out_specs = (P("rep", "feat", None), P("feat", None), P("feat", None))
    return jax.shard_map(body, mesh=mesh, in_specs=in_specs, out_specs=out_specs, check_vma=False)
```

```python
import functools

import jax
import jax.numpy as jnp
from jax import lax
from jax.experimental import pallas as pl
from jax.experimental.pallas import tpu as pltpu
from jax.sharding import PartitionSpec as P

MESH = pl.DeviceIdType.MESH
SIDE = 4
PLANE = 2 * SIDE * SIDE
STEP = (0, 1, 3, 2)
F32 = jnp.float32
BF16 = jnp.bfloat16


def remote(src, dst, send_sem, recv_sem, axis, index):
    return pltpu.make_async_remote_copy(
        src_ref=src,
        dst_ref=dst,
        send_sem=send_sem,
        recv_sem=recv_sem,
        device_id={axis: index},
        device_id_type=MESH,
    )


def exchange_kernel(
    reps,
    slots,
    src_hbm,
    count_hbm,
    order_hbm,
    feats_hbm,
    tiles_hbm,
    w_self_hbm,
    w_neigh_hbm,
    bias_hbm,
    cot_hbm,
    hidden_out,
    total_out,
    src_ref,
    count_ref,
    order_ref,
    feats,
    tiles,
    means,
    mine,
    rows,
    weights,
    grads,
    cot,
    bias,
    hidden,
    part,
    near,
    far,
    whole,
    load_sems,
    feat_sems,
    tile_sems,
    out_sems,
    ready_sems,
    a2a_send,
    a2a_recv,
    w_send,
    w_recv,
    g_send,
    g_recv,
    z_send,
    z_recv,
):
    me = lax.axis_index("feat")
    z = lax.axis_index("rep")
    x, y, c = me // (2 * SIDE), (me // 2) % SIDE, me % 2
    blocks = tiles.shape[0]
    chunks = tile_sems.shape[0]
    chunk = blocks // chunks

    barrier = pltpu.get_barrier_semaphore()

    at_x = [lax.rem(x + d, SIDE) * (2 * SIDE) for d in range(SIDE)]
    at_y = [lax.rem(y + d, SIDE) * 2 for d in range(SIDE)]
    at_c = [c, 1 - c]
    at_a = [at_x[d] * (1 - c) + at_y[d] * c for d in STEP]
    at_b = [at_x[d] * c + at_y[d] * (1 - c) for d in STEP]
    from_a = [at_x[-d % SIDE] * (1 - c) + at_y[-d % SIDE] * c for d in STEP]
    from_b = [at_x[-d % SIDE] * c + at_y[-d % SIDE] * (1 - c) for d in STEP]
    at = lambda a, b, dc: at_a[a] + at_b[b] + at_c[dc]
    partner = at(0, 0, 1)
    along = lambda o: lax.rem(z + reps + o, reps)

    def signal(sem, axis, index):
        pl.semaphore_signal(sem, inc=1, device_id={axis: index}, device_id_type=MESH)

    for k in (1, 2, 3):
        signal(barrier, "feat", at(k, 0, 0))
        signal(barrier, "feat", at(0, k, 0))
    signal(barrier, "feat", partner)
    for o in (1, -1, 2, -2):
        signal(barrier, "rep", along(o))

    index_loads = [
        pltpu.make_async_copy(src_hbm, src_ref, load_sems.at[5]),
        pltpu.make_async_copy(count_hbm, count_ref, load_sems.at[6]),
        pltpu.make_async_copy(order_hbm, order_ref, load_sems.at[7]),
    ]
    w_loads = [
        pltpu.make_async_copy(w_self_hbm, weights.at[0, pl.ds(0, 32)], load_sems.at[0]),
        pltpu.make_async_copy(w_neigh_hbm, weights.at[0, pl.ds(32, 32)], load_sems.at[1]),
    ]
    feat_loads = [
        pltpu.make_async_copy(
            feats_hbm.at[i], feats.at[:, pl.ds(i * 8, 8)], feat_sems.at[i]
        )
        for i in range(4)
    ]
    small_loads = [
        pltpu.make_async_copy(bias_hbm, bias, load_sems.at[3]),
        pltpu.make_async_copy(cot_hbm, cot, load_sems.at[4]),
    ]

    def tile_load(i):
        piece = pl.ds(i * chunk, chunk)
        return pltpu.make_async_copy(tiles_hbm.at[piece], tiles.at[piece], tile_sems.at[i])

    for load in w_loads + index_loads:
        load.start()
    tile_load(0).start()
    for load in feat_loads:
        load.start()
    for i in range(1, chunks):
        tile_load(i).start()
    for load in small_loads:
        load.start()

    class Gather:
        def __init__(self, buffer, send, recv):
            self.buffer, self.send, self.recv = buffer, send, recv
            self.sent, self.spans = [], {}

        def go(self, source, count, target, index):
            copy = remote(
                self.buffer.at[pl.ds(source, count)],
                self.buffer.at[pl.ds(target, count)],
                self.send.at[len(self.sent)],
                self.recv.at[len(self.sent)],
                "feat",
                index,
            )
            copy.start()
            self.spans[target] = len(self.sent)
            self.sent.append(copy)

        def got(self, *targets):
            for target in targets:
                self.sent[self.spans[target]].wait_recv()

        def along_a(self):
            for a in (1, 2, 3):
                self.go(0, 1, a, at(a, 0, 0))

        def along_b(self, first, count):
            for b in (1, 2, 3):
                self.go(first, count, 4 * b + first, at(0, b, 0))

        def cross(self, first, count):
            self.go(first, count, 16 + first, partner)

        def drain(self):
            for copy in self.sent:
                copy.wait_send()

    for load in w_loads:
        load.wait()
    pl.semaphore_wait(barrier, 11)
    w_gather = Gather(weights, w_send, w_recv)
    w_gather.along_a()
    for k in (1, 2, 3):
        signal(ready_sems.at[k], "feat", at(k, 0, 0))
    signal(ready_sems.at[4], "rep", along(2))
    signal(ready_sems.at[5], "rep", along(-2))

    for load in index_loads + feat_loads:
        load.wait()

    def combine(i, carry):
        tile_load(i).wait()
        for b in range(chunk):
            block = i * chunk + b
            used = count_ref[0, block]
            left = jnp.concatenate(
                [
                    feats[src_ref[k, 0, block]] * (k < used).astype(F32).astype(BF16)
                    for k in range(slots)
                ],
                axis=1,
            )
            right = jnp.concatenate([tiles[block, k] for k in range(slots)], axis=1)
            means[block] = lax.dot_general(
                left, right, (((1,), (1,)), ((), ())), preferred_element_type=F32
            ).astype(BF16)
        return carry

    lax.fori_loop(0, chunks - 1, combine, 0)
    for k in (1, 2, 3):
        pl.semaphore_wait(ready_sems.at[k], 1)
    signal(ready_sems.at[0], "feat", partner)
    w_gather.got(1, 2, 3)
    w_gather.along_b(0, 4)
    w_gather.cross(0, 4)
    lax.fori_loop(chunks - 1, chunks, combine, 0)

    def arrange(p, carry):
        block = order_ref[0, p]
        mine[p, 0:32, :] = feats[block]
        mine[p, 32:64, :] = means[block]
        return carry

    lax.fori_loop(0, PLANE, arrange, 0, unroll=4)

    pl.semaphore_wait(ready_sems.at[0], 1)
    for dc in range(2):
        for b in range(SIDE):
            for a in range(SIDE):
                slot = 16 * dc + 4 * b + a
                if slot:
                    target = at(a, b, dc)
                    remote(
                        mine.at[target], rows.at[slot], a2a_send, a2a_recv.at[slot], "feat", target
                    ).start()
    for i in (4, 5):
        pl.semaphore_wait(ready_sems.at[i], 1)
    signal(ready_sems.at[6], "rep", along(4))
    signal(ready_sems.at[7], "rep", along(-4))
    rows[0] = mine[me]
    for load in small_loads:
        load.wait()

    for b in (1, 2, 3):
        w_gather.got(4 * b)
        w_gather.cross(4 * b, 4)
    preact = jnp.broadcast_to(bias[...], (128, 256))
    for g in range(8):
        if g >= 4:
            w_gather.got(4 * g)
        for d in range(4 * g, 4 * g + 4):
            if d:
                remote(
                    rows.at[d], rows.at[d], a2a_send, a2a_recv.at[d], "feat", partner
                ).wait_recv()
        left = rows[4 * g : 4 * g + 4].reshape(256, 128)
        right = weights[4 * g : 4 * g + 4].reshape(256, 256)
        preact = preact + lax.dot_general(
            left, right, (((0,), (0,)), ((), ())), preferred_element_type=F32
        )
    squash = jax.nn.sigmoid(preact)
    slope = cot[...].astype(F32) * squash * (1.0 + preact * (1.0 - squash))
    grads[0] = slope.astype(BF16)
    g_gather = Gather(grads, g_send, g_recv)
    g_gather.along_a()
    g_gather.along_b(0, 1)
    hidden[...] = (preact * squash).astype(BF16)
    hidden_copy = pltpu.make_async_copy(hidden, hidden_out, out_sems.at[0])
    hidden_copy.start()

    def owner(slot):
        dc, b, a = slot // 16, slot // 4 % 4, slot % 4
        return (from_b[a] + from_a[b] if dc else from_a[a] + from_b[b]) + at_c[dc]

    def terms(group):
        result = jnp.zeros((64, 256), F32)
        for i in range(0, len(group), 2):
            pair = group[i : i + 2]
            left = jnp.concatenate([mine[owner(slot)] for slot in pair], axis=1)
            right = jnp.concatenate([grads[slot] for slot in pair], axis=0)
            result = result + jnp.dot(left, right, preferred_element_type=F32)
        return result

    g_gather.got(1, 2)
    g_gather.along_b(1, 2)
    g_gather.got(3)
    g_gather.along_b(3, 1)
    g_gather.cross(0, 4)
    grad = terms([0, 1, 2, 3])
    for b in (1, 2, 3):
        g_gather.got(4 * b, 4 * b + 1)
        g_gather.cross(4 * b, 3)
    grad = grad + terms([4, 5, 6, 8, 9, 10, 12, 13, 14])
    for b in (1, 2, 3):
        g_gather.got(4 * b + 3)
        g_gather.cross(4 * b + 3, 1)
    g_gather.got(16, 20, 24, 28)
    grad = grad + terms([16, 17, 18, 19, 20, 21, 22, 24, 25, 26, 28, 29, 30])
    grad = grad + terms([7, 11, 15])
    g_gather.got(23, 27, 31)
    grad = grad + terms([23, 27, 31])

    for row in range(8):
        for col in range(2):
            piece = row * 2 + col
            part[piece // 4, piece % 4] = grad[row * 8 : row * 8 + 8, col * 128 : col * 128 + 128]

    sent = []

    def send_rep(source, target, offset):
        copy = remote(
            source,
            target,
            z_send.at[len(sent)],
            z_recv.at[len(sent)],
            "rep",
            lax.rem(z + reps + offset, reps),
        )
        copy.start()
        sent.append(copy)

    for o in (2, 1, -1):
        send_rep(part.at[lax.rem(z + 4 + o, 4)], near.at[o % 4], o)
    for copy in sent[0:3]:
        copy.wait_recv()
    far[z // 4] = (part[lax.rem(z, 4)] + near[2]) + (near[1] + near[3])
    pl.semaphore_wait(ready_sems.at[6], 1)
    pl.semaphore_wait(ready_sems.at[7], 1)
    for o in (8, 4, -4):
        send_rep(far.at[z // 4], far.at[z // 4], o)
    for i, o in enumerate((8, 4, -4)):
        slot = far.at[lax.rem(z + reps - o, reps) // 4]
        remote(slot, slot, z_send.at[3 + i], z_recv.at[3 + i], "rep", z).wait_recv()
    whole[...] = (far[0] + far[1]) + (far[2] + far[3])
    for o in (2, 1, -1):
        send_rep(whole, total_out.at[o % 4], o)
    own = pltpu.make_async_copy(whole, total_out.at[0], out_sems.at[1])
    own.start()

    for copy in sent[0:6]:
        copy.wait_send()
    all_rows = pl.ds(1, PLANE - 1)
    remote(
        mine.at[all_rows], mine.at[all_rows], a2a_send, a2a_recv.at[0], "feat", partner
    ).wait_send()
    w_gather.drain()
    g_gather.drain()
    hidden_copy.wait()
    own.wait()
    for copy in sent[6:9]:
        copy.wait()


def finish_kernel(hidden_in, total_in, hidden_ref, grad_self_ref, grad_neigh_ref):
    z = lax.axis_index("rep")
    hidden_ref[0] = hidden_in[...]
    for piece in range(16):
        row, col = piece // 2, piece % 2
        value = total_in[lax.rem(z + 4 - piece // 4, 4), piece % 4]
        target = grad_self_ref if row < 4 else grad_neigh_ref
        target[row % 4 * 8 : row % 4 * 8 + 8, col * 128 : col * 128 + 128] = value


def solution(mesh):
    reps = mesh.shape["rep"]

    def body(feats, w_self, w_neigh, bias, tile_weight, tile_src, tile_count, owner_order, cotangent):
        slots = tile_weight.shape[2]
        vmem = pl.BlockSpec(memory_space=pltpu.VMEM)
        anywhere = pl.BlockSpec(memory_space=pl.ANY)
        dma = pltpu.SemaphoreType.DMA
        hidden, total = pl.pallas_call(
            functools.partial(exchange_kernel, reps, slots),
            out_shape=(
                jax.ShapeDtypeStruct((128, 256), BF16),
                jax.ShapeDtypeStruct((4, 4, 8, 128), F32),
            ),
            in_specs=[anywhere] * 9,
            out_specs=(anywhere, anywhere),
            scratch_shapes=[
                pltpu.SMEM((slots, 1, 32), jnp.int32),
                pltpu.SMEM((1, 32), jnp.int32),
                pltpu.SMEM((1, 32), jnp.int32),
                pltpu.VMEM((64, 32, 128), BF16),
                pltpu.VMEM((32, slots, 128, 128), BF16),
                pltpu.VMEM((32, 32, 128), BF16),
                pltpu.VMEM((PLANE, 64, 128), BF16),
                pltpu.VMEM((PLANE, 64, 128), BF16),
                pltpu.VMEM((PLANE, 64, 256), BF16),
                pltpu.VMEM((PLANE, 128, 256), BF16),
                pltpu.VMEM((128, 256), BF16),
                pltpu.VMEM((1, 256), F32),
                pltpu.VMEM((128, 256), BF16),
                pltpu.VMEM((4, 4, 8, 128), F32),
                pltpu.VMEM((4, 4, 8, 128), F32),
                pltpu.VMEM((4, 4, 8, 128), F32),
                pltpu.VMEM((4, 8, 128), F32),
                dma((8,)),
                dma((4,)),
                dma((8,)),
                dma((2,)),
                pltpu.SemaphoreType.REGULAR((8,)),
                dma,
                dma((PLANE,)),
                dma((10,)),
                dma((10,)),
                dma((19,)),
                dma((19,)),
                dma((9,)),
                dma((9,)),
            ],
            compiler_params=pltpu.CompilerParams(collective_id=0, has_side_effects=True),
            name="exchange",
        )(
            tile_src.transpose(2, 0, 1),
            tile_count,
            owner_order,
            feats[0].T.reshape(4, 8, 64, 128).transpose(0, 2, 1, 3),
            tile_weight[0],
            w_self,
            w_neigh,
            bias.reshape(1, -1),
            cotangent[0],
        )
        return pl.pallas_call(
            finish_kernel,
            out_shape=(
                jax.ShapeDtypeStruct((1, 128, 256), BF16),
                jax.ShapeDtypeStruct((32, 256), F32),
                jax.ShapeDtypeStruct((32, 256), F32),
            ),
            in_specs=[vmem] * 2,
            out_specs=(vmem,) * 3,
            name="finish",
        )(hidden, total)

    in_specs = (
        P("rep", None, "feat"),
        P("feat", None),
        P("feat", None),
        P(),
        P("rep", None, None, None, None),
        P("rep", None, None),
        P("rep", None),
        P("rep", None),
        P("rep", "feat", None),
    )
    out_specs = (P("rep", "feat", None), P("feat", None), P("feat", None))
    return jax.shard_map(body, mesh=mesh, in_specs=in_specs, out_specs=out_specs, check_vma=False)
```

```python
import functools

import jax
import jax.numpy as jnp
from jax import lax
from jax.experimental import pallas as pl
from jax.experimental.pallas import tpu as pltpu
from jax.sharding import PartitionSpec as P

MESH = pl.DeviceIdType.MESH
SIDE = 4
PLANE = 2 * SIDE * SIDE
F32 = jnp.float32
BF16 = jnp.bfloat16


def remote(src, dst, send_sem, recv_sem, axis, index):
    return pltpu.make_async_remote_copy(
        src_ref=src,
        dst_ref=dst,
        send_sem=send_sem,
        recv_sem=recv_sem,
        device_id={axis: index},
        device_id_type=MESH,
    )


def exchange_kernel(
    reps,
    slots,
    src_hbm,
    count_hbm,
    order_hbm,
    feats_hbm,
    tiles_hbm,
    w_self_hbm,
    w_neigh_hbm,
    bias_hbm,
    cot_hbm,
    hidden_out,
    total_out,
    src_ref,
    count_ref,
    order_ref,
    feats,
    tiles,
    means,
    mine,
    rows,
    weights,
    grads,
    cot,
    bias,
    hidden,
    mine_part,
    part,
    near,
    far,
    whole,
    load_sems,
    feat_sems,
    tile_sems,
    out_sems,
    ready_sems,
    a2a_send,
    a2a_recv,
    w_send,
    w_recv,
    g_send,
    g_recv,
    z_send,
    z_recv,
):
    me = lax.axis_index("feat")
    z = lax.axis_index("rep")
    x, y, c = me // (2 * SIDE), (me // 2) % SIDE, me % 2
    blocks = tiles.shape[0]
    chunks = tile_sems.shape[0]
    chunk = blocks // chunks

    barrier = pltpu.get_barrier_semaphore()

    at_x = [lax.rem(x + d, SIDE) * (2 * SIDE) for d in range(SIDE)]
    at_y = [lax.rem(y + d, SIDE) * 2 for d in range(SIDE)]
    at_c = [c, 1 - c]
    at = lambda dx, dy, dc: at_x[dx % SIDE] + at_y[dy % SIDE] + at_c[dc]
    first = lambda k: (k * (1 - c) * SIDE + k * c) * 2
    second = lambda k: (k * c * SIDE + k * (1 - c)) * 2
    first_at = lambda k: at(k, 0, 0) * (1 - c) + at(0, k, 0) * c
    second_at = lambda k: at(k, 0, 0) * c + at(0, k, 0) * (1 - c)
    partner = at(0, 0, 1)
    near_first = (1, 3, 2)
    along = lambda o: lax.rem(z + reps + o, reps)

    def signal(sem, axis, index):
        pl.semaphore_signal(sem, inc=1, device_id={axis: index}, device_id_type=MESH)

    for k in near_first:
        signal(barrier, "feat", at(k, 0, 0))
        signal(barrier, "feat", at(0, k, 0))
    signal(barrier, "feat", partner)
    for o in (1, -1, 2, -2):
        signal(barrier, "rep", along(o))

    index_loads = [
        pltpu.make_async_copy(src_hbm, src_ref, load_sems.at[5]),
        pltpu.make_async_copy(count_hbm, count_ref, load_sems.at[6]),
        pltpu.make_async_copy(order_hbm, order_ref, load_sems.at[7]),
    ]
    w_loads = [
        pltpu.make_async_copy(w_self_hbm, weights.at[0, pl.ds(0, 32)], load_sems.at[0]),
        pltpu.make_async_copy(w_neigh_hbm, weights.at[0, pl.ds(32, 32)], load_sems.at[1]),
    ]
    feat_loads = [
        pltpu.make_async_copy(
            feats_hbm.at[i], feats.at[:, pl.ds(i * 8, 8)], feat_sems.at[i]
        )
        for i in range(4)
    ]
    small_loads = [
        pltpu.make_async_copy(bias_hbm, bias, load_sems.at[3]),
        pltpu.make_async_copy(cot_hbm, cot, load_sems.at[4]),
    ]

    def tile_load(i):
        piece = pl.ds(i * chunk, chunk)
        return pltpu.make_async_copy(tiles_hbm.at[piece], tiles.at[piece], tile_sems.at[i])

    for load in w_loads + index_loads:
        load.start()
    tile_load(0).start()
    for load in feat_loads:
        load.start()
    for i in range(1, chunks):
        tile_load(i).start()
    for load in small_loads:
        load.start()

    class Gather:
        def __init__(self, buffer, send, recv, cuts):
            self.buffer, self.send, self.recv, self.cuts = buffer, send, recv, cuts
            self.height = buffer.shape[1] // cuts
            self.sent = []

        def ref(self, slot, h):
            return self.buffer.at[slot, pl.ds(h * self.height, self.height)]

        def go(self, source, target, h, index):
            copy = remote(
                self.ref(source, h),
                self.ref(target, h),
                self.send.at[len(self.sent)],
                self.recv.at[target * self.cuts + h],
                "feat",
                index,
            )
            copy.start()
            self.sent.append(copy)

        def got(self, slot, h):
            ref = self.ref(slot, h)
            sem = self.recv.at[slot * self.cuts + h]
            remote(ref, ref, self.send.at[0], sem, "feat", partner).wait_recv()

        def stage_one(self):
            for h in range(self.cuts):
                for k in near_first:
                    self.go(0, first(k), h, first_at(k))
            for h in range(self.cuts):
                for k in near_first:
                    self.go(0, second(k), h, second_at(k))
            for h in range(self.cuts):
                self.go(0, 1, h, partner)

        def forward(self, k, h):
            self.got(first(k), h)
            for j in near_first:
                self.go(first(k), first(k) + second(j), h, second_at(j))
            self.go(first(k), first(k) + 1, h, partner)

        def cross(self, slot, h):
            self.got(slot, h)
            self.go(slot, slot + 1, h, partner)

        def take(self, slot):
            for h in range(self.cuts):
                self.got(slot, h)

        def drain(self):
            for copy in self.sent:
                copy.wait_send()

    for load in w_loads:
        load.wait()
    pl.semaphore_wait(barrier, 11)
    w_gather = Gather(weights, w_send, w_recv, 1)
    w_gather.stage_one()
    for k in near_first:
        signal(ready_sems.at[k], "feat", first_at(k))
    signal(ready_sems.at[4], "rep", along(2))
    signal(ready_sems.at[5], "rep", along(-2))

    for load in index_loads + feat_loads:
        load.wait()

    def combine(i, carry):
        tile_load(i).wait()
        for b in range(chunk):
            block = i * chunk + b
            used = count_ref[0, block]
            left = jnp.concatenate(
                [
                    feats[src_ref[k, 0, block]] * (k < used).astype(F32).astype(BF16)
                    for k in range(slots)
                ],
                axis=1,
            )
            right = jnp.concatenate([tiles[block, k] for k in range(slots)], axis=1)
            means[block] = lax.dot_general(
                left, right, (((1,), (1,)), ((), ())), preferred_element_type=F32
            ).astype(BF16)
        return carry

    lax.fori_loop(0, chunks - 1, combine, 0)
    for k in near_first:
        pl.semaphore_wait(ready_sems.at[k], 1)
    signal(ready_sems.at[0], "feat", partner)
    for k in near_first:
        w_gather.forward(k, 0)
    lax.fori_loop(chunks - 1, chunks, combine, 0)

    def arrange(p, carry):
        block = order_ref[0, p]
        mine[p, 0:32, :] = feats[block]
        mine[p, 32:64, :] = means[block]
        return carry

    lax.fori_loop(0, PLANE, arrange, 0, unroll=4)

    pl.semaphore_wait(ready_sems.at[0], 1)
    for d in list(range(16, 24)) + list(range(8, 16)) + list(range(24, 32)) + list(range(1, 8)):
        target = at(d // (2 * SIDE), d // 2 % SIDE, d % 2)
        remote(
            mine.at[target], rows.at[d], a2a_send, a2a_recv.at[d], "feat", target
        ).start()
    for i in (4, 5):
        pl.semaphore_wait(ready_sems.at[i], 1)
    signal(ready_sems.at[6], "rep", along(4))
    signal(ready_sems.at[7], "rep", along(-4))
    rows[0] = mine[me]
    for load in small_loads:
        load.wait()

    for k in near_first:
        w_gather.cross(second(k), 0)
    for k in near_first:
        for j in near_first:
            w_gather.cross(first(k) + second(j), 0)
    for s in range(SIDE * SIDE):
        w_gather.take(2 * s + 1)

    preact = jnp.broadcast_to(bias[...], (128, 256))
    for g in (0, 1, 2, 3, 6, 7, 4, 5):
        for d in range(4 * g, 4 * g + 4):
            if d:
                remote(
                    rows.at[d], rows.at[d], a2a_send, a2a_recv.at[d], "feat", partner
                ).wait_recv()
        left = rows[4 * g : 4 * g + 4].reshape(256, 128)
        right = weights[4 * g : 4 * g + 4].reshape(256, 256)
        preact = preact + lax.dot_general(
            left, right, (((0,), (0,)), ((), ())), preferred_element_type=F32
        )
    squash = jax.nn.sigmoid(preact)
    slope = cot[...].astype(F32) * squash * (1.0 + preact * (1.0 - squash))
    grads[0] = slope.astype(BF16)
    g_gather = Gather(grads, g_send, g_recv, 2)
    g_gather.stage_one()
    hidden[...] = (preact * squash).astype(BF16)
    hidden_copy = pltpu.make_async_copy(hidden, hidden_out, out_sems.at[0])
    hidden_copy.start()

    def owner(slot):
        dx, dy, dc = slot // (2 * SIDE), lax.rem(slot // 2, SIDE), lax.rem(slot, 2)
        return (
            lax.rem(x + SIDE - dx, SIDE) * (2 * SIDE)
            + lax.rem(y + SIDE - dy, SIDE) * 2
            + lax.rem(c + dc, 2)
        )

    def terms(group):
        result = jnp.zeros((64, 256), F32)
        for i in range(0, len(group), 2):
            pair = group[i : i + 2]
            left = jnp.concatenate([mine[owner(slot)] for slot in pair], axis=1)
            right = jnp.concatenate([grads[slot] for slot in pair], axis=0)
            result = result + jnp.dot(left, right, preferred_element_type=F32)
        return result

    corners = [(k, j) for k in near_first for j in near_first]
    for h in range(2):
        for k in near_first:
            g_gather.forward(k, h)
    for h in range(2):
        for k in near_first:
            g_gather.cross(second(k), h)
    straight = [side(k) for k in near_first for side in (first, second)]
    grad = terms([jnp.int32(0)] + straight)
    g_gather.take(1)
    for slot in straight:
        g_gather.take(slot + 1)
    grad = grad + terms([jnp.int32(1)] + [slot + 1 for slot in straight])
    for h in range(2):
        for k, j in corners:
            g_gather.cross(first(k) + second(j), h)
    grad = grad + terms([first(k) + second(j) for k, j in corners])
    last = [second(k) + first(j) + 1 for k, j in corners]
    for slot in last:
        g_gather.take(slot)
    grad = grad + terms(last)

    for row in range(8):
        for col in range(2):
            piece = row * 2 + col
            value = grad[row * 8 : row * 8 + 8, col * 128 : col * 128 + 128]
            mine_part[piece // 4, piece % 4] = value
            part[piece // 4, piece % 4] = value.astype(BF16)

    sent = []

    def send_rep(source, target, offset):
        copy = remote(
            source,
            target,
            z_send.at[len(sent)],
            z_recv.at[len(sent)],
            "rep",
            lax.rem(z + reps + offset, reps),
        )
        copy.start()
        sent.append(copy)

    for o in (2, 1, -1):
        send_rep(part.at[lax.rem(z + 4 + o, 4)], near.at[o % 4], o)
    for copy in sent[0:3]:
        copy.wait_recv()
    wide = lambda value: value.astype(F32)
    window = (mine_part[lax.rem(z, 4)] + wide(near[2])) + (wide(near[1]) + wide(near[3]))
    far[z // 4] = window.astype(BF16)
    pl.semaphore_wait(ready_sems.at[6], 1)
    pl.semaphore_wait(ready_sems.at[7], 1)
    for o in (8, 4, -4):
        send_rep(far.at[z // 4], far.at[z // 4], o)
    for i, o in enumerate((8, 4, -4)):
        slot = far.at[lax.rem(z + reps - o, reps) // 4]
        remote(slot, slot, z_send.at[3 + i], z_recv.at[3 + i], "rep", z).wait_recv()
    whole[...] = (wide(far[0]) + wide(far[1])) + (wide(far[2]) + wide(far[3]))
    for o in (2, 1, -1):
        send_rep(whole, total_out.at[o % 4], o)
    own = pltpu.make_async_copy(whole, total_out.at[0], out_sems.at[1])
    own.start()

    for copy in sent[0:6]:
        copy.wait_send()
    all_rows = pl.ds(1, PLANE - 1)
    remote(
        mine.at[all_rows], mine.at[all_rows], a2a_send, a2a_recv.at[0], "feat", partner
    ).wait_send()
    w_gather.drain()
    g_gather.drain()
    hidden_copy.wait()
    own.wait()
    for copy in sent[6:9]:
        copy.wait()


def finish_kernel(hidden_in, total_in, hidden_ref, grad_self_ref, grad_neigh_ref):
    z = lax.axis_index("rep")
    hidden_ref[0] = hidden_in[...]
    for piece in range(16):
        row, col = piece // 2, piece % 2
        value = total_in[lax.rem(z + 4 - piece // 4, 4), piece % 4]
        target = grad_self_ref if row < 4 else grad_neigh_ref
        target[row % 4 * 8 : row % 4 * 8 + 8, col * 128 : col * 128 + 128] = value


def solution(mesh):
    reps = mesh.shape["rep"]

    def body(feats, w_self, w_neigh, bias, tile_weight, tile_src, tile_count, owner_order, cotangent):
        slots = tile_weight.shape[2]
        vmem = pl.BlockSpec(memory_space=pltpu.VMEM)
        anywhere = pl.BlockSpec(memory_space=pl.ANY)
        dma = pltpu.SemaphoreType.DMA
        hidden, total = pl.pallas_call(
            functools.partial(exchange_kernel, reps, slots),
            out_shape=(
                jax.ShapeDtypeStruct((128, 256), BF16),
                jax.ShapeDtypeStruct((4, 4, 8, 128), F32),
            ),
            in_specs=[anywhere] * 9,
            out_specs=(anywhere, anywhere),
            scratch_shapes=[
                pltpu.SMEM((slots, 1, 32), jnp.int32),
                pltpu.SMEM((1, 32), jnp.int32),
                pltpu.SMEM((1, 32), jnp.int32),
                pltpu.VMEM((64, 32, 128), BF16),
                pltpu.VMEM((32, slots, 128, 128), BF16),
                pltpu.VMEM((32, 32, 128), BF16),
                pltpu.VMEM((PLANE, 64, 128), BF16),
                pltpu.VMEM((PLANE, 64, 128), BF16),
                pltpu.VMEM((PLANE, 64, 256), BF16),
                pltpu.VMEM((PLANE, 128, 256), BF16),
                pltpu.VMEM((128, 256), BF16),
                pltpu.VMEM((1, 256), F32),
                pltpu.VMEM((128, 256), BF16),
                pltpu.VMEM((4, 4, 8, 128), F32),
                pltpu.VMEM((4, 4, 8, 128), BF16),
                pltpu.VMEM((4, 4, 8, 128), BF16),
                pltpu.VMEM((4, 4, 8, 128), BF16),
                pltpu.VMEM((4, 8, 128), F32),
                dma((8,)),
                dma((4,)),
                dma((8,)),
                dma((2,)),
                pltpu.SemaphoreType.REGULAR((8,)),
                dma,
                dma((PLANE,)),
                dma((PLANE,)),
                dma((PLANE,)),
                dma((2 * PLANE,)),
                dma((2 * PLANE,)),
                dma((9,)),
                dma((9,)),
            ],
            compiler_params=pltpu.CompilerParams(collective_id=0, has_side_effects=True),
            name="exchange",
        )(
            tile_src.transpose(2, 0, 1),
            tile_count,
            owner_order,
            feats[0].T.reshape(4, 8, 64, 128).transpose(0, 2, 1, 3),
            tile_weight[0],
            w_self,
            w_neigh,
            bias.reshape(1, -1),
            cotangent[0],
        )
        return pl.pallas_call(
            finish_kernel,
            out_shape=(
                jax.ShapeDtypeStruct((1, 128, 256), BF16),
                jax.ShapeDtypeStruct((32, 256), F32),
                jax.ShapeDtypeStruct((32, 256), F32),
            ),
            in_specs=[vmem] * 2,
            out_specs=(vmem,) * 3,
            name="finish",
        )(hidden, total)

    in_specs = (
        P("rep", None, "feat"),
        P("feat", None),
        P("feat", None),
        P(),
        P("rep", None, None, None, None),
        P("rep", None, None),
        P("rep", None),
        P("rep", None),
        P("rep", "feat", None),
    )
    out_specs = (P("rep", "feat", None), P("feat", None), P("feat", None))
    return jax.shard_map(body, mesh=mesh, in_specs=in_specs, out_specs=out_specs, check_vma=False)
```

```python
import functools

import jax
import jax.numpy as jnp
from jax import lax
from jax.experimental import pallas as pl
from jax.experimental.pallas import tpu as pltpu
from jax.sharding import PartitionSpec as P

MESH = pl.DeviceIdType.MESH
SIDE = 4
PLANE = 2 * SIDE * SIDE
F32 = jnp.float32
BF16 = jnp.bfloat16


def remote(src, dst, send_sem, recv_sem, axis, index):
    return pltpu.make_async_remote_copy(
        src_ref=src,
        dst_ref=dst,
        send_sem=send_sem,
        recv_sem=recv_sem,
        device_id={axis: index},
        device_id_type=MESH,
    )


def exchange_kernel(
    reps,
    slots,
    src_hbm,
    count_hbm,
    order_hbm,
    feats_hbm,
    tiles_hbm,
    w_self_hbm,
    w_neigh_hbm,
    bias_hbm,
    cot_hbm,
    hidden_out,
    total_out,
    src_ref,
    count_ref,
    order_ref,
    feats,
    tiles,
    means,
    mine,
    rows,
    weights,
    grads,
    cot,
    bias,
    hidden,
    mine_part,
    part,
    near,
    far,
    whole,
    load_sems,
    feat_sems,
    tile_sems,
    out_sems,
    ready_sems,
    a2a_send,
    a2a_recv,
    w_send,
    w_recv,
    g_send,
    g_recv,
    z_send,
    z_recv,
):
    me = lax.axis_index("feat")
    z = lax.axis_index("rep")
    x, y, c = me // (2 * SIDE), (me // 2) % SIDE, me % 2
    blocks = tiles.shape[0]
    chunks = tile_sems.shape[0]
    chunk = blocks // chunks

    barrier = pltpu.get_barrier_semaphore()

    at_x = [lax.rem(x + d, SIDE) * (2 * SIDE) for d in range(SIDE)]
    at_y = [lax.rem(y + d, SIDE) * 2 for d in range(SIDE)]
    at_c = [c, 1 - c]
    at = lambda dx, dy, dc: at_x[dx % SIDE] + at_y[dy % SIDE] + at_c[dc]
    first = lambda k: (k * (1 - c) * SIDE + k * c) * 2
    second = lambda k: (k * c * SIDE + k * (1 - c)) * 2
    first_at = lambda k: at(k, 0, 0) * (1 - c) + at(0, k, 0) * c
    second_at = lambda k: at(k, 0, 0) * c + at(0, k, 0) * (1 - c)
    partner = at(0, 0, 1)
    near_first = (1, 3, 2)
    along = lambda o: lax.rem(z + reps + o, reps)

    def signal(sem, axis, index):
        pl.semaphore_signal(sem, inc=1, device_id={axis: index}, device_id_type=MESH)

    for k in near_first:
        signal(barrier, "feat", at(k, 0, 0))
        signal(barrier, "feat", at(0, k, 0))
    signal(barrier, "feat", partner)
    for o in (1, -1, 2, -2):
        signal(barrier, "rep", along(o))

    index_loads = [
        pltpu.make_async_copy(src_hbm, src_ref, load_sems.at[5]),
        pltpu.make_async_copy(count_hbm, count_ref, load_sems.at[6]),
        pltpu.make_async_copy(order_hbm, order_ref, load_sems.at[7]),
    ]
    w_loads = [
        pltpu.make_async_copy(w_self_hbm, weights.at[0, pl.ds(0, 32)], load_sems.at[0]),
        pltpu.make_async_copy(w_neigh_hbm, weights.at[0, pl.ds(32, 32)], load_sems.at[1]),
    ]
    feat_loads = [
        pltpu.make_async_copy(
            feats_hbm.at[i], feats.at[:, pl.ds(i * 8, 8)], feat_sems.at[i]
        )
        for i in range(4)
    ]
    small_loads = [
        pltpu.make_async_copy(bias_hbm, bias, load_sems.at[3]),
        pltpu.make_async_copy(cot_hbm, cot, load_sems.at[4]),
    ]

    def tile_load(i):
        piece = pl.ds(i * chunk, chunk)
        return pltpu.make_async_copy(tiles_hbm.at[piece], tiles.at[piece], tile_sems.at[i])

    for load in w_loads + index_loads:
        load.start()
    tile_load(0).start()
    for load in feat_loads:
        load.start()
    for i in range(1, chunks):
        tile_load(i).start()
    for load in small_loads:
        load.start()

    class Gather:
        def __init__(self, buffer, send, recv, cuts):
            self.buffer, self.send, self.recv, self.cuts = buffer, send, recv, cuts
            self.height = buffer.shape[1] // cuts
            self.sent = []

        def ref(self, slot, h):
            return self.buffer.at[slot, pl.ds(h * self.height, self.height)]

        def go(self, source, target, h, index):
            copy = remote(
                self.ref(source, h),
                self.ref(target, h),
                self.send.at[len(self.sent)],
                self.recv.at[target * self.cuts + h],
                "feat",
                index,
            )
            copy.start()
            self.sent.append(copy)

        def got(self, slot, h):
            ref = self.ref(slot, h)
            sem = self.recv.at[slot * self.cuts + h]
            remote(ref, ref, self.send.at[0], sem, "feat", partner).wait_recv()

        def stage_one(self):
            for h in range(self.cuts):
                for k in near_first:
                    self.go(0, first(k), h, first_at(k))
            for h in range(self.cuts):
                for k in near_first:
                    self.go(0, second(k), h, second_at(k))
            for h in range(self.cuts):
                self.go(0, 1, h, partner)

        def forward(self, k, h):
            self.got(first(k), h)
            for j in near_first:
                self.go(first(k), first(k) + second(j), h, second_at(j))
            self.go(first(k), first(k) + 1, h, partner)

        def cross(self, slot, h):
            self.got(slot, h)
            self.go(slot, slot + 1, h, partner)

        def take(self, slot):
            for h in range(self.cuts):
                self.got(slot, h)

        def drain(self):
            for copy in self.sent:
                copy.wait_send()

    for load in w_loads:
        load.wait()
    pl.semaphore_wait(barrier, 11)
    w_gather = Gather(weights, w_send, w_recv, 1)
    w_gather.stage_one()
    for k in near_first:
        signal(ready_sems.at[k], "feat", first_at(k))
    signal(ready_sems.at[4], "rep", along(2))
    signal(ready_sems.at[5], "rep", along(-2))

    for load in index_loads + feat_loads:
        load.wait()

    def combine(i, carry):
        tile_load(i).wait()
        for b in range(chunk):
            block = i * chunk + b
            used = count_ref[0, block]
            left = jnp.concatenate(
                [
                    feats[src_ref[k, 0, block]] * (k < used).astype(F32).astype(BF16)
                    for k in range(slots)
                ],
                axis=1,
            )
            right = jnp.concatenate([tiles[block, k] for k in range(slots)], axis=1)
            means[block] = lax.dot_general(
                left, right, (((1,), (1,)), ((), ())), preferred_element_type=F32
            ).astype(BF16)
        return carry

    lax.fori_loop(0, chunks - 1, combine, 0)
    for k in near_first:
        pl.semaphore_wait(ready_sems.at[k], 1)
    signal(ready_sems.at[0], "feat", partner)
    lax.fori_loop(chunks - 1, chunks, combine, 0)

    def arrange(p, carry):
        block = order_ref[0, p]
        mine[p, 0:32, :] = feats[block]
        mine[p, 32:64, :] = means[block]
        return carry

    lax.fori_loop(0, PLANE, arrange, 0, unroll=4)

    pl.semaphore_wait(ready_sems.at[0], 1)
    for d in range(1, 32):
        target = at(d // (2 * SIDE), d // 2 % SIDE, d % 2)
        remote(
            mine.at[target], rows.at[d], a2a_send, a2a_recv.at[d], "feat", target
        ).start()
    for k in near_first:
        w_gather.forward(k, 0)
    for i in (4, 5):
        pl.semaphore_wait(ready_sems.at[i], 1)
    signal(ready_sems.at[6], "rep", along(4))
    signal(ready_sems.at[7], "rep", along(-4))
    rows[0] = mine[me]
    for load in small_loads:
        load.wait()

    for k in near_first:
        w_gather.cross(second(k), 0)
    for k in near_first:
        for j in near_first:
            w_gather.cross(first(k) + second(j), 0)
    for s in range(SIDE * SIDE):
        w_gather.take(2 * s + 1)

    preact = jnp.broadcast_to(bias[...], (128, 256))
    for g in (0, 1, 2, 3, 6, 7, 4, 5):
        for d in range(4 * g, 4 * g + 4):
            if d:
                remote(
                    rows.at[d], rows.at[d], a2a_send, a2a_recv.at[d], "feat", partner
                ).wait_recv()
        left = rows[4 * g : 4 * g + 4].reshape(256, 128)
        right = weights[4 * g : 4 * g + 4].reshape(256, 256)
        preact = preact + lax.dot_general(
            left, right, (((0,), (0,)), ((), ())), preferred_element_type=F32
        )
    squash = jax.nn.sigmoid(preact)
    slope = cot[...].astype(F32) * squash * (1.0 + preact * (1.0 - squash))
    grads[0] = slope.astype(BF16)
    g_gather = Gather(grads, g_send, g_recv, 2)
    g_gather.stage_one()
    hidden[...] = (preact * squash).astype(BF16)
    hidden_copy = pltpu.make_async_copy(hidden, hidden_out, out_sems.at[0])
    hidden_copy.start()

    def owner(slot):
        dx, dy, dc = slot // (2 * SIDE), lax.rem(slot // 2, SIDE), lax.rem(slot, 2)
        return (
            lax.rem(x + SIDE - dx, SIDE) * (2 * SIDE)
            + lax.rem(y + SIDE - dy, SIDE) * 2
            + lax.rem(c + dc, 2)
        )

    def terms(group):
        result = jnp.zeros((64, 256), F32)
        for i in range(0, len(group), 2):
            pair = group[i : i + 2]
            left = jnp.concatenate([mine[owner(slot)] for slot in pair], axis=1)
            right = jnp.concatenate([grads[slot] for slot in pair], axis=0)
            result = result + jnp.dot(left, right, preferred_element_type=F32)
        return result

    corners = [(k, j) for k in near_first for j in near_first]
    for h in range(2):
        for k in near_first:
            g_gather.forward(k, h)
    for h in range(2):
        for k in near_first:
            g_gather.cross(second(k), h)
    straight = [side(k) for k in near_first for side in (first, second)]
    grad = terms([jnp.int32(0)] + straight)
    g_gather.take(1)
    for slot in straight:
        g_gather.take(slot + 1)
    grad = grad + terms([jnp.int32(1)] + [slot + 1 for slot in straight])
    for h in range(2):
        for k, j in corners:
            g_gather.cross(first(k) + second(j), h)
    grad = grad + terms([first(k) + second(j) for k, j in corners])
    last = [second(k) + first(j) + 1 for k, j in corners]
    for slot in last:
        g_gather.take(slot)
    grad = grad + terms(last)

    for row in range(8):
        for col in range(2):
            piece = row * 2 + col
            value = grad[row * 8 : row * 8 + 8, col * 128 : col * 128 + 128]
            mine_part[piece // 4, piece % 4] = value
            part[piece // 4, piece % 4] = value.astype(BF16)

    sent = []

    def send_rep(source, target, offset):
        copy = remote(
            source,
            target,
            z_send.at[len(sent)],
            z_recv.at[len(sent)],
            "rep",
            lax.rem(z + reps + offset, reps),
        )
        copy.start()
        sent.append(copy)

    for o in (2, 1, -1):
        send_rep(part.at[lax.rem(z + 4 + o, 4)], near.at[o % 4], o)
    for copy in sent[0:3]:
        copy.wait_recv()
    wide = lambda value: value.astype(F32)
    window = (mine_part[lax.rem(z, 4)] + wide(near[2])) + (wide(near[1]) + wide(near[3]))
    far[z // 4] = window.astype(BF16)
    pl.semaphore_wait(ready_sems.at[6], 1)
    pl.semaphore_wait(ready_sems.at[7], 1)
    for o in (8, 4, -4):
        send_rep(far.at[z // 4], far.at[z // 4], o)
    for i, o in enumerate((8, 4, -4)):
        slot = far.at[lax.rem(z + reps - o, reps) // 4]
        remote(slot, slot, z_send.at[3 + i], z_recv.at[3 + i], "rep", z).wait_recv()
    whole[...] = (wide(far[0]) + wide(far[1])) + (wide(far[2]) + wide(far[3]))
    for o in (2, 1, -1):
        send_rep(whole, total_out.at[o % 4], o)
    own = pltpu.make_async_copy(whole, total_out.at[0], out_sems.at[1])
    own.start()

    for copy in sent[0:6]:
        copy.wait_send()
    all_rows = pl.ds(1, PLANE - 1)
    remote(
        mine.at[all_rows], mine.at[all_rows], a2a_send, a2a_recv.at[0], "feat", partner
    ).wait_send()
    w_gather.drain()
    g_gather.drain()
    hidden_copy.wait()
    own.wait()
    for copy in sent[6:9]:
        copy.wait()


def finish_kernel(hidden_in, total_in, hidden_ref, grad_self_ref, grad_neigh_ref):
    z = lax.axis_index("rep")
    hidden_ref[0] = hidden_in[...]
    for piece in range(16):
        row, col = piece // 2, piece % 2
        value = total_in[lax.rem(z + 4 - piece // 4, 4), piece % 4]
        target = grad_self_ref if row < 4 else grad_neigh_ref
        target[row % 4 * 8 : row % 4 * 8 + 8, col * 128 : col * 128 + 128] = value


def solution(mesh):
    reps = mesh.shape["rep"]

    def body(feats, w_self, w_neigh, bias, tile_weight, tile_src, tile_count, owner_order, cotangent):
        slots = tile_weight.shape[2]
        vmem = pl.BlockSpec(memory_space=pltpu.VMEM)
        anywhere = pl.BlockSpec(memory_space=pl.ANY)
        dma = pltpu.SemaphoreType.DMA
        hidden, total = pl.pallas_call(
            functools.partial(exchange_kernel, reps, slots),
            out_shape=(
                jax.ShapeDtypeStruct((128, 256), BF16),
                jax.ShapeDtypeStruct((4, 4, 8, 128), F32),
            ),
            in_specs=[anywhere] * 9,
            out_specs=(anywhere, anywhere),
            scratch_shapes=[
                pltpu.SMEM((slots, 1, 32), jnp.int32),
                pltpu.SMEM((1, 32), jnp.int32),
                pltpu.SMEM((1, 32), jnp.int32),
                pltpu.VMEM((64, 32, 128), BF16),
                pltpu.VMEM((32, slots, 128, 128), BF16),
                pltpu.VMEM((32, 32, 128), BF16),
                pltpu.VMEM((PLANE, 64, 128), BF16),
                pltpu.VMEM((PLANE, 64, 128), BF16),
                pltpu.VMEM((PLANE, 64, 256), BF16),
                pltpu.VMEM((PLANE, 128, 256), BF16),
                pltpu.VMEM((128, 256), BF16),
                pltpu.VMEM((1, 256), F32),
                pltpu.VMEM((128, 256), BF16),
                pltpu.VMEM((4, 4, 8, 128), F32),
                pltpu.VMEM((4, 4, 8, 128), BF16),
                pltpu.VMEM((4, 4, 8, 128), BF16),
                pltpu.VMEM((4, 4, 8, 128), BF16),
                pltpu.VMEM((4, 8, 128), F32),
                dma((8,)),
                dma((4,)),
                dma((8,)),
                dma((2,)),
                pltpu.SemaphoreType.REGULAR((8,)),
                dma,
                dma((PLANE,)),
                dma((PLANE,)),
                dma((PLANE,)),
                dma((2 * PLANE,)),
                dma((2 * PLANE,)),
                dma((9,)),
                dma((9,)),
            ],
            compiler_params=pltpu.CompilerParams(collective_id=0, has_side_effects=True),
            name="exchange",
        )(
            tile_src.transpose(2, 0, 1),
            tile_count,
            owner_order,
            feats[0].T.reshape(4, 8, 64, 128).transpose(0, 2, 1, 3),
            tile_weight[0],
            w_self,
            w_neigh,
            bias.reshape(1, -1),
            cotangent[0],
        )
        return pl.pallas_call(
            finish_kernel,
            out_shape=(
                jax.ShapeDtypeStruct((1, 128, 256), BF16),
                jax.ShapeDtypeStruct((32, 256), F32),
                jax.ShapeDtypeStruct((32, 256), F32),
            ),
            in_specs=[vmem] * 2,
            out_specs=(vmem,) * 3,
            name="finish",
        )(hidden, total)

    in_specs = (
        P("rep", None, "feat"),
        P("feat", None),
        P("feat", None),
        P(),
        P("rep", None, None, None, None),
        P("rep", None, None),
        P("rep", None),
        P("rep", None),
        P("rep", "feat", None),
    )
    out_specs = (P("rep", "feat", None), P("feat", None), P("feat", None))
    return jax.shard_map(body, mesh=mesh, in_specs=in_specs, out_specs=out_specs, check_vma=False)
```
